512 devices in a mesh: beam: 16 (over y, x), ma: 32 (over z, core).
Axes of the slice: x: 4, y: 4, z: 16, core: 2. Of those that a mesh axis runs over, the one named last changes fastest.
Arguments:
- sky_harmonics: float32 [64, 2, 2048], P('ma'), may hold values from -6 to 6
- beam_harmonics: float32 [128, 2, 2048], P('beam'), may hold values from -6 to 6
- wigner: bfloat16 [128, 64, 64, 2048], P('beam', 'ma'), may hold values from -0.125 to 0.125
- order_map: int32 [64], replicated, may hold values from 0 to 2047, as said below
- block_owner: int32 [4096, 1], P('ma'), may hold values from 0 to 31; in each aligned block of 128 rows (0 to 127, 128 to 255, ...) at most 8 rows name the same one
- block_local: int32 [4096], P('ma'), may hold values from 0 to 63
- cell_offset: int32 [524288], P('ma'), may hold values from 0 to 126
- cell_fraction: float32 [524288], P('ma'), may hold values from 0 to 1
- beam_angle: float32 [524288], P('ma'), may hold values from -3.140625 to 3.140625
- sample_count: int32 [32], P('ma'), may hold values from 1 to 16384, 393216 in all
- noise_weight: float32 [128, 128], replicated, may hold values from -0.2 to 2, as said below
Outputs:
- sky_gradient: float32 [64, 2, 2048], P('ma', None, 'beam')
The draws below stay inside these ranges and needn't reach their ends.
Inputs may be any that keep to these rules, and one draw needn't show every extreme that they name: `order_map`: 64 distinct azimuthal orders. `block_owner`: among the 128 sample blocks of one device, at most 8 name the same owner, and in some device some owner is named exactly 8 times. `noise_weight`: diagonal entries lie in 1 to 2, the others within 0.2 in magnitude.
All inputs are finite; a program needn't handle non-finite values. No bound on the sum of `sample_count` on one device may be relied on, other than what follows from the above.
Results may differ from the reference program's by a relative error of at most 0.017.
Values may be sent and summed in bfloat16 or wider, within the bound.
A program may use at most 128 MiB of HBM per device.

```python
import math
import jax
import jax.numpy as jnp
import numpy as np
from jax import lax

L = 2048
PHI = 4096
CELLS = 128
NSB = 128
K = 128
M = 64
R = 64
BLK_DEV = 64
S_DEV = 16384
SB_ALL = 4096
S_ALL = 524288
CAP = 8
N_MA = 32


def draw_order_map(key, part):
    return jax.random.permutation(key, L)[:M].astype(jnp.int32)


def draw_noise_weight(key, part):
    first_key, second_key = jax.random.split(jax.random.fold_in(key, 17))
    diagonal = jax.random.uniform(first_key, (CELLS,), jnp.float32, 1.0, 2.0)
    spread_part = jax.random.normal(second_key, (CELLS, CELLS), jnp.float32) * (0.5 / jnp.sqrt(CELLS * 1.0))
    spread_part = jnp.clip(spread_part, -0.2, 0.2)
    eye_mask = jnp.eye(CELLS, dtype=jnp.float32)
    return (jnp.diag(diagonal) + spread_part * (1.0 - eye_mask)).astype(jnp.float32)


def plant(entries, rng, least, high):
    longest = entries.shape.index(max(entries.shape))
    spots = []
    for shift in (0, 1):
        where = [jax.random.randint(jax.random.fold_in(rng, axis), (), 0, length) for axis, length in enumerate(entries.shape)]
        where[longest] = (where[longest] + shift) % entries.shape[longest]
        spots.append(tuple(where))
    return entries.at[spots[0]].set(least).at[spots[1]].set(high)


def steps_of(rng, shape, shards, low, largest):
    gain = 1.0
    for dim, parts in shards:
        heights = jax.random.uniform(jax.random.fold_in(jax.random.fold_in(rng, 6), dim), (parts,), jnp.float32, low / len(shards), largest / len(shards))
        gain = gain * jnp.repeat(jnp.exp(heights), shape[dim] // parts).reshape((-1,) + (1,) * (len(shape) - 1 - dim))
    return gain


def length_profile(number_of, total, most, skew):
    weights = [(1 << 20) // math.isqrt(rank ** skew) + 1 for rank in range(2, number_of + 1)]
    surplus, given = total - most - (number_of - 1), [1] * (number_of - 1)
    while surplus > 0:
        free = [i for i in range(number_of - 1) if given[i] < most]
        pool, budget = sum([weights[i] for i in free]), surplus
        for i in free:
            addition = min(most - given[i], max(1, budget * weights[i] // pool), surplus)
            given[i] = given[i] + addition
            surplus = surplus - addition
    return np.array([most] + given)


def ragged_sizes(rng, number_of, total, bound, lean):
    if number_of == 2:
        one = jax.random.randint(rng, (), max(1, total - bound), min(bound, total - 1) + 1)
        return jnp.stack([one, total - one])
    tallies = jnp.asarray(length_profile(number_of, total, bound, lean), jnp.int32)
    couples = (number_of - 1) // 2
    source_of, taker = tallies[1:1 + 2 * couples:2], tallies[2:2 + 2 * couples:2]
    slack = jnp.minimum(source_of - 1, bound - taker)
    moved = jax.random.randint(jax.random.fold_in(rng, 1), (couples,), 0, 1 << 20) % (slack + 1)
    tallies = tallies.at[1:1 + 2 * couples:2].set(source_of - moved).at[2:2 + 2 * couples:2].set(taker + moved)
    return tallies[jax.random.permutation(jax.random.fold_in(rng, 2), number_of)]


def routed_block(own_key, own, number, rows, amount, top, bound, slope):
    ranking = jax.random.permutation(own_key, amount)
    heavy_load, ordinary = load_shares(amount, rows * top, bound, slope, True), load_shares(amount, rows * top, bound, slope, False)
    places = jnp.arange(amount)

    def named(sizes, offset_by):
        used = int((sizes > 0).sum())
        fixed = max(1, used // 4)
        shifted = fixed + (places - fixed + offset_by * (used - fixed)) % max(1, amount - fixed)
        return jnp.zeros((amount,), jnp.int32).at[ranking[jnp.where(places < fixed, places, shifted)]].set(jnp.asarray(sizes, jnp.int32))

    sizes = jnp.where(number % 4 == 0, named(heavy_load, number // 4), named(ordinary, number - number // 4 - 1))
    mixed = jax.random.permutation(jax.random.fold_in(own, 3), amount)
    giver, sink = mixed[0:amount // 2 * 2:2], mixed[1:amount // 2 * 2:2]
    slack = jnp.minimum(sizes[giver] - 1, bound - sizes[sink]) // 2
    slack = jnp.where((giver == ranking[0]) | (sink == ranking[0]) | (sizes[sink] == 0), 0, jnp.maximum(slack, 0))
    shifted = jax.random.randint(jax.random.fold_in(own, 4), (amount // 2,), 0, 1 << 20) % (slack + 1)
    sizes = sizes.at[giver].add(-shifted).at[sink].add(shifted)
    items = jnp.searchsorted(jnp.cumsum(sizes), jnp.arange(rows * top), side="right").astype(jnp.int32)
    table = items.reshape(top, rows).T
    table = table[jax.random.permutation(jax.random.fold_in(own, 1), rows)]
    offset_by = jax.random.randint(jax.random.fold_in(own, 2), (rows, 1), 0, top)
    return jnp.take_along_axis(table, (jnp.arange(top)[None, :] + offset_by) % top, axis=1)


def load_shares(count, total, bound, lean, full):
    weights = [(1 << 20) // math.isqrt(grade ** lean) + 1 for grade in range(1, count + 1)]
    largest = bound if full else min(bound, max(-(-total // count), total * weights[0] // sum(weights)))
    least = 1 if total - largest >= count - 1 else 0
    given, surplus = [largest] + [least] * (count - 1), total - largest - least * (count - 1)
    while surplus > 0:
        candidates = [i for i in range(1, count) if given[i] < largest] or [i for i in range(1, count) if given[i] < bound]
        pool, remaining = sum([weights[i] for i in candidates]), surplus
        for i in candidates:
            addition = min(bound - given[i], max(1, remaining * weights[i] // pool), surplus)
            given[i] = given[i] + addition
            surplus = surplus - addition
    return np.array(given)


def scatter_about(key, dims, scale, limit, pieces=(), kind=jnp.bfloat16):
    entries = jax.random.normal(key, dims, jnp.float32) * scale
    if len(pieces) > 0:
        entries = steps_of(key, dims, pieces, -0.22, 0.18) * entries
    return jnp.clip(entries, min=-limit, max=limit).astype(kind)


def setup_inputs(seed: int = 0) -> dict:
    splits = jax.random.split(jax.random.key(seed), 12)
    sky_harmonics = scatter_about(splits[0], (M, 2, L), 1.0, 6.0, ((0, 32),), jnp.float32)
    beam_harmonics = scatter_about(splits[1], (K, 2, L), 1.0, 6.0, ((0, 16),), jnp.float32)
    wigner = scatter_about(splits[2], (K, M, R, L), L ** -0.5, 0.125, ((0, 16), (1, 32)))
    order_map = draw_order_map(jax.random.fold_in(splits[11], 71), 0)
    block_owner_keys = jax.random.split(jax.random.fold_in(splits[4], 1), SB_ALL // NSB)
    block_owner_turns = jax.random.permutation(jax.random.fold_in(splits[4], 3), SB_ALL // NSB)
    block_owner = jax.vmap(lambda own, number: routed_block(jax.random.fold_in(splits[4], 2), own, number, NSB, N_MA, 1, CAP, 2))(block_owner_keys, block_owner_turns).reshape((SB_ALL, 1))
    block_local = plant(jax.random.randint(splits[5], (SB_ALL,), 0, BLK_DEV), jax.random.fold_in(splits[5], 1), 0, BLK_DEV - 1).astype(jnp.int32)
    cell_offset = plant(jax.random.randint(splits[6], (S_ALL,), 0, CELLS - 1), jax.random.fold_in(splits[6], 1), 0, (CELLS - 1) - 1).astype(jnp.int32)
    cell_fraction = jnp.clip(1.0 * jax.random.uniform(splits[7], (S_ALL,), jnp.float32) ** steps_of(splits[7], (S_ALL,), ((0, 32),), -0.2, 0.2), 0.0, 1.0)
    beam_angle = jnp.clip(jax.random.uniform(splits[8], (S_ALL,), jnp.float32, -3.140625, 3.140625), -3.140625, 3.140625)
    sample_count = ragged_sizes(splits[9], N_MA, N_MA * S_DEV * 3 // 4, S_DEV, 2).astype(jnp.int32)
    noise_weight = draw_noise_weight(jax.random.fold_in(splits[11], 71), 0)
    return dict(sky_harmonics=sky_harmonics, beam_harmonics=beam_harmonics, wigner=wigner, order_map=order_map, block_owner=block_owner, block_local=block_local, cell_offset=cell_offset, cell_fraction=cell_fraction, beam_angle=beam_angle, sample_count=sample_count, noise_weight=noise_weight)


def cycle_phases(order_map, cycle_cells):
    stepped = jnp.arange(cycle_cells, dtype=jnp.int32)
    phase_turns = order_map[:, None] * stepped[None, :] % cycle_cells
    angles = phase_turns.astype(jnp.float32) * (2.0 * math.pi / cycle_cells)
    scaling = 1.0 / math.sqrt(order_map.shape[0])
    return jnp.stack([jnp.cos(angles), -jnp.sin(angles)], axis=1) * scaling

def rotation(beam_order, beam_angle, total_orders):
    spin_order = ((beam_order + 1) // 2).astype(jnp.float32)
    angles = spin_order * beam_angle
    return jnp.where(beam_order % 2 == 0, jnp.cos(angles), jnp.sin(angles)) / math.sqrt(total_orders)

def harmonic_product(sky_harmonics, beam_harmonics):
    sky_real = sky_harmonics[None, :, 0]
    sky_imag = sky_harmonics[None, :, 1]
    beam_real = beam_harmonics[:, None, 0]
    beam_imag = beam_harmonics[:, None, 1]
    first = sky_real * beam_real - sky_imag * beam_imag
    second = sky_real * beam_imag + sky_imag * beam_real
    return jnp.stack([first, second], axis=2).astype(jnp.bfloat16)

def gradient_terms(grad_harmonics, beam_harmonics):
    grad_real = grad_harmonics[:, :, 0]
    grad_imag = grad_harmonics[:, :, 1]
    beam_real = beam_harmonics[:, None, 0]
    beam_imag = beam_harmonics[:, None, 1]
    first = lax.optimization_barrier(jnp.sum(grad_real * beam_real + grad_imag * beam_imag, axis=0))
    second = lax.optimization_barrier(jnp.sum(grad_imag * beam_real - grad_real * beam_imag, axis=0))
    return jnp.stack([first, second], axis=1)

def reference(sky_harmonics, beam_harmonics, wigner, order_map, block_owner, block_local, cell_offset, cell_fraction, beam_angle, sample_count, noise_weight):
    highest = lax.Precision.HIGHEST
    total_orders = beam_harmonics.shape[0]
    phase_table = cycle_phases(order_map, PHI)
    block_index = block_owner[:, 0] * BLK_DEV + block_local
    cell_low = jnp.repeat(block_index, CELLS) * CELLS + cell_offset
    cell_high = cell_low + 1
    stamps = jnp.arange(cell_offset.shape[0], dtype=jnp.int32)
    valid_mask = (stamps % S_DEV < sample_count[stamps // S_DEV]).astype(jnp.float32)

    def forward_step(beam_order, signal):
        beam_order = jnp.asarray(beam_order).astype(jnp.int32)
        beam_row = lax.dynamic_slice_in_dim(beam_harmonics, beam_order, 1, 0)
        table_row = lax.dynamic_index_in_dim(wigner, beam_order, 0, keepdims=False).astype(jnp.float32)
        product = harmonic_product(sky_harmonics, beam_row)[0].astype(jnp.float32)
        cycle_modes = jnp.einsum('mcl,mrl->mcr', product, table_row, precision=highest)
        cube_flat = jnp.einsum('mcr,mcp->rp', cycle_modes, phase_table, precision=highest).reshape(-1)
        values = (1.0 - cell_fraction) * cube_flat[cell_low] + cell_fraction * cube_flat[cell_high]
        return signal + rotation(beam_order, beam_angle, total_orders) * values
    signal = lax.fori_loop(0, total_orders, forward_step, jnp.zeros(cell_offset.shape, jnp.float32))
    signal = signal * valid_mask
    filtered = jnp.einsum('bu,tu->bt', signal.reshape(-1, CELLS), noise_weight, precision=highest).reshape(-1) * valid_mask

    def adjoint_step(beam_order, gradient):
        beam_order = jnp.asarray(beam_order).astype(jnp.int32)
        beam_row = lax.dynamic_slice_in_dim(beam_harmonics, beam_order, 1, 0)
        table_row = lax.dynamic_index_in_dim(wigner, beam_order, 0, keepdims=False).astype(jnp.float32)
        weighted = rotation(beam_order, beam_angle, total_orders) * filtered
        cube_grad = jnp.zeros((R * PHI,), jnp.float32)
        cube_grad = cube_grad.at[cell_low].add((1.0 - cell_fraction) * weighted)
        cube_grad = cube_grad.at[cell_high].add(cell_fraction * weighted)
        grad_modes = jnp.einsum('rp,mcp->mcr', cube_grad.reshape(R, PHI), phase_table, precision=highest).astype(jnp.bfloat16)
        grad_harmonics = jnp.einsum('mcr,mrl->mcl', grad_modes.astype(jnp.float32), table_row, precision=highest)
        return gradient + gradient_terms(grad_harmonics[None], beam_row)
    return lax.fori_loop(0, total_orders, adjoint_step, jnp.zeros(sky_harmonics.shape, jnp.float32))
```

```python
import functools
import math

import jax
import jax.numpy as jnp
from jax import lax
from jax.experimental import pallas as pl
from jax.experimental.pallas import tpu as pltpu
from jax.sharding import PartitionSpec as P

F32 = jnp.float32
BF16 = jnp.bfloat16
I32 = jnp.int32

COS_TURNS = (
    0.99999997389483,
    -19.739202931827737,
    64.93907559492132,
    -85.44969773655134,
    60.1656143595228,
    -25.96416606164654,
    6.528151014475474,
)
N_MA = 32
N_BEAM = 16
KL = 8
PHI_BLOCKS = 32
NSB = 128


def cos_turns(turns):
    v = turns - jnp.floor(turns + 0.5)
    w = v * v
    acc = jnp.full_like(w, COS_TURNS[-1])
    for coef in COS_TURNS[-2::-1]:
        acc = acc * w + coef
    return acc


def nn(a, b):
    return lax.dot_general(a, b, (((1,), (0,)), ((), ())), preferred_element_type=F32)


def nt(a, b):
    return lax.dot_general(a, b, (((1,), (1,)), ((), ())), preferred_element_type=F32)


def split(x):
    high = x.astype(BF16)
    return high, (x - high.astype(F32)).astype(BF16)


def kernel(
    owner_s,
    local_s,
    order_s,
    count_s,
    owner_ref,
    local_ref,
    sky_hbm,
    beam_hbm,
    wig_hbm,
    offset_hbm,
    fraction_hbm,
    angle_hbm,
    noise_hbm,
    out_ref,
    sky,
    beam,
    wig,
    offset,
    fraction,
    angle,
    noise,
    order,
    phase,
    turn,
    interp,
    rows,
    piece,
    gathered,
    gathered_f,
    modes,
    partial,
    signals,
    filtered,
    gmat,
    gout_f,
    gout,
    gin,
    fin,
    fin_in,
    load_sem,
    wig_sem,
    ag_send,
    ag_recv,
    rs_send,
    rs_recv,
    fl_send,
    fl_recv,
    gr_send,
    gr_recv,
    fin_send,
    fin_recv,
):
    me_a = lax.axis_index("ma")
    me_b = lax.axis_index("beam")

    loads = [
        pltpu.make_async_copy(src, dst, load_sem.at[i])
        for i, (src, dst) in enumerate(
            [
                (beam_hbm, beam),
                (sky_hbm, sky),
                (offset_hbm, offset),
                (fraction_hbm, fraction),
                (angle_hbm, angle),
                (noise_hbm, noise),
            ]
        )
    ]
    wig_loads = [
        pltpu.make_async_copy(wig_hbm.at[pl.ds(2 * i, 2)], wig.at[pl.ds(2 * i, 2)], wig_sem.at[i])
        for i in range(4)
    ]
    loads[0].start()
    loads[1].start()
    for copy in wig_loads:
        copy.start()
    for copy in loads[2:]:
        copy.start()

    barrier = pltpu.get_barrier_semaphore()

    def greet_ma(i, _):
        pl.semaphore_signal(barrier, inc=1, device_id={"ma": lax.rem(me_a + i, N_MA)})
        return 0

    def greet_beam(i, _):
        pl.semaphore_signal(barrier, inc=1, device_id={"beam": lax.rem(me_b + i, N_BEAM)})
        return 0

    lax.fori_loop(1, N_MA, greet_ma, 0)
    lax.fori_loop(1, N_BEAM, greet_beam, 0)

    def far_first(i):
        half = (i + 1) // 2
        return lax.rem(me_a + N_MA + 16 + half * (1 - 2 * lax.rem(i, 2)), N_MA)

    def copy_ma(src, dst, send, recv, peer):
        return pltpu.make_async_remote_copy(
            src_ref=src,
            dst_ref=dst,
            send_sem=send.at[peer],
            recv_sem=recv.at[me_a],
            device_id={"ma": peer},
        )

    def copy_beam(src, dst, send, recv, peer):
        return pltpu.make_async_remote_copy(
            src_ref=src,
            dst_ref=dst,
            send_sem=send.at[peer],
            recv_sem=recv.at[me_b],
            device_id={"beam": peer},
        )

    def came(dst, send, recv, source):
        return pltpu.make_async_remote_copy(
            src_ref=dst,
            dst_ref=dst,
            send_sem=send.at[source],
            recv_sem=recv.at[source],
            device_id={"ma": me_a},
        )

    loads[0].wait()
    loads[1].wait()
    beam_re = beam[:, 0, :]
    beam_im = beam[:, 1, :]
    products = []
    for m in range(2):
        sky_re = sky[m, 0:1, :]
        sky_im = sky[m, 1:2, :]
        products.append(
            jnp.concatenate(
                [sky_re * beam_re - sky_im * beam_im, sky_re * beam_im + sky_im * beam_re], axis=0
            ).astype(BF16)
        )
    sub = lax.broadcasted_iota(I32, (KL, 128), 0)
    lane = lax.broadcasted_iota(I32, (KL, 128), 1)
    for quad in range(2):
        wig_loads[2 * quad].wait()
        wig_loads[2 * quad + 1].wait()
        for m in range(2):
            weights = jnp.concatenate([wig[4 * quad + k, m] for k in range(4)], axis=0)
            out = nt(products[m], weights)
            for pair in range(2):
                kp = 2 * quad + pair
                keep = sub == 2 * kp + lane // 64
                for c in range(2):
                    part = out[c * KL : (c + 1) * KL, pair * 128 : (pair + 1) * 128]
                    row = (m * 2 + c) * 4 + kp
                    rows[row : row + 1, :] = jnp.sum(
                        jnp.where(keep, part, 0.0), axis=0, keepdims=True
                    )
    piece[...] = rows[...].astype(BF16)

    pl.semaphore_wait(barrier, N_MA - 1 + N_BEAM - 1)

    def send_modes(i, _):
        copy_ma(piece, gathered.at[me_a], ag_send, ag_recv, far_first(i)).start()
        return 0

    lax.fori_loop(0, N_MA - 1, send_modes, 0)
    gathered[me_a] = piece[...]

    for copy in loads[2:]:
        copy.wait()
    for m in range(64):
        order[2 * m : 2 * m + 2, :] = jnp.full((2, 128), order_s[m], I32)
    quarter = (lax.broadcasted_iota(I32, (128, 128), 0) % 2).astype(F32) * 0.25

    def phases(b, _):
        cells = (b * 128 + lax.broadcasted_iota(I32, (128, 128), 1)).astype(F32) * (1.0 / 4096.0)
        turns = order[...].astype(F32) * cells + quarter
        high, low = split(cos_turns(turns) * 0.125)
        phase[b] = jnp.concatenate([high, low], axis=1)
        return 0

    lax.fori_loop(0, PHI_BLOCKS, phases, 0)

    beam_order = me_b * KL + sub
    spin = ((beam_order + 1) // 2).astype(F32)
    back = (beam_order % 2).astype(F32) * 0.25

    def turns_of(s, _):
        around = angle[pl.ds(s, 1), :] * (1.0 / (2.0 * math.pi))
        turn[s] = cos_turns(spin * around - back) * (1.0 / math.sqrt(128.0))
        return 0

    lax.fori_loop(0, NSB, turns_of, 0, unroll=4)

    cell = lax.broadcasted_iota(I32, (128, 128), 0)

    def interpolators(s, _):
        block = lax.rem(local_s[s], PHI_BLOCKS)
        low = offset[pl.ds(s, 1), :]
        right = fraction[pl.ds(s, 1), :]
        mix = jnp.where(
            cell == low, 1.0 - right, jnp.where(cell == low + 1, right, 0.0)
        ).astype(BF16)
        interp[s] = nn(phase[block], jnp.concatenate([mix, mix], axis=0)).astype(BF16)
        return 0

    lax.fori_loop(0, NSB, interpolators, 0, unroll=4)

    def modes_arrive(i, _):
        source = far_first(N_MA - 2 - i)
        came(gathered.at[source], ag_send, ag_recv, source).wait_recv()
        return 0

    lax.fori_loop(0, N_MA - 1, modes_arrive, 0)
    gathered_f[...] = gathered[...].astype(F32).reshape(512, 128)
    for kp in range(4):
        block = gathered_f[pl.ds(kp, 128, stride=4), :].T
        modes[:, 2 * kp, :] = block[:64]
        modes[:, 2 * kp + 1, :] = block[64:]

    def octet(i, _):
        peer = lax.rem(me_b + 1 + i, N_BEAM)
        for j in range(8):
            s = peer * 8 + j
            cycle = owner_s[s] * 2 + lax.div(local_s[s], PHI_BLOCKS)
            own = modes[cycle].astype(BF16)
            values = nn(own, interp[s])
            partial[peer, j : j + 1, :] = jnp.sum(turn[s] * values, axis=0, keepdims=True)

        @pl.when(i < N_BEAM - 1)
        def _():
            copy_beam(partial.at[peer], signals.at[me_b], rs_send, rs_recv, peer).start()

        return 0

    lax.fori_loop(0, N_BEAM, octet, 0)

    def signals_arrive(i, total):
        source = lax.rem(me_b + N_BEAM - 1 - i, N_BEAM)
        came(signals.at[source], rs_send, rs_recv, source).wait_recv()
        return total + signals[source]

    total = lax.fori_loop(0, N_BEAM - 1, signals_arrive, partial[me_b])
    stamps = (
        (me_b * 8 + lax.broadcasted_iota(I32, (8, 128), 0)) * 128
        + lax.broadcasted_iota(I32, (8, 128), 1)
    )
    valid = (stamps < count_s[0]).astype(F32)
    filtered[me_b] = (
        lax.dot_general(
            total * valid,
            noise[...],
            (((1,), (1,)), ((), ())),
            precision=lax.Precision.HIGHEST,
            preferred_element_type=F32,
        )
        * valid
    )

    def send_filtered(i, _):
        peer = lax.rem(me_b + 1 + i, N_BEAM)
        copy_beam(filtered.at[me_b], filtered.at[me_b], fl_send, fl_recv, peer).start()
        return 0

    lax.fori_loop(0, N_BEAM - 1, send_filtered, 0)

    def adjoint(i, _):
        source = lax.rem(me_b + N_BEAM - i, N_BEAM)

        @pl.when(i > 0)
        def _():
            came(filtered.at[source], fl_send, fl_recv, source).wait_recv()

        eight = filtered[source]
        for j in range(8):
            s = source * 8 + j
            high, low = split(turn[s] * eight[j : j + 1, :])
            both = nt(jnp.concatenate([high, low], axis=0), interp[s])
            gmat[pl.ds(pl.multiple_of(s * KL, KL), KL), :] = both[:KL] + both[KL:]
        return 0

    lax.fori_loop(0, N_BEAM, adjoint, 0)

    cycles = owner_ref[...] * 2 + lax.div(local_ref[...], jnp.full((1, NSB), PHI_BLOCKS, I32))
    pick = (lax.broadcasted_iota(I32, (64, 128), 0) == cycles).astype(F32).astype(BF16)
    pick = jnp.concatenate([pick, pick], axis=1)
    for kp in range(4):
        halves = []
        for k in (2 * kp, 2 * kp + 1):
            high, low = split(gmat[pl.ds(k, 128, stride=KL), :])
            halves.append(nn(pick, jnp.concatenate([high, low], axis=0)))
        gout_f[pl.ds(kp, 128, stride=4), :] = jnp.concatenate(halves, axis=0).T
    gout[...] = gout_f[...].reshape(N_MA, 16, 128).astype(BF16)

    def send_grads(i, _):
        peer = far_first(i)
        copy_ma(gout.at[peer], gin.at[me_a], gr_send, gr_recv, peer).start()
        return 0

    lax.fori_loop(0, N_MA - 1, send_grads, 0)

    def grads_arrive(i, acc):
        source = far_first(N_MA - 2 - i)
        came(gin.at[source], gr_send, gr_recv, source).wait_recv()
        return acc + gin[source].astype(F32)

    rows[...] = lax.fori_loop(0, N_MA - 1, grads_arrive, gout[me_a].astype(F32))

    for m in range(2):
        lhs = []
        for c in range(2):
            for kp in range(4):
                row = (m * 2 + c) * 4 + kp
                spreadout = jnp.broadcast_to(rows[row : row + 1, :], (KL, 128))
                lhs.append(jnp.where(sub == 2 * kp + lane // 64, spreadout, 0.0))
        lhs = jnp.concatenate(
            [jnp.concatenate(lhs[:4], axis=1), jnp.concatenate(lhs[4:], axis=1)], axis=0
        ).astype(BF16)
        weights = jnp.concatenate([wig[k, m] for k in range(KL)], axis=0)
        harm = nn(lhs, weights)
        re, im = harm[:KL], harm[KL:]
        first = jnp.sum(re * beam_re + im * beam_im, axis=0, keepdims=True)
        second = jnp.sum(im * beam_re - re * beam_im, axis=0, keepdims=True)
        for b in range(N_BEAM):
            fin[b, 2 * m : 2 * m + 1, :] = first[:, b * 128 : (b + 1) * 128]
            fin[b, 2 * m + 1 : 2 * m + 2, :] = second[:, b * 128 : (b + 1) * 128]

    def send_final(i, _):
        peer = lax.rem(me_b + 1 + i, N_BEAM)
        copy_beam(fin.at[peer], fin_in.at[me_b], fin_send, fin_recv, peer).start()
        return 0

    lax.fori_loop(0, N_BEAM - 1, send_final, 0)

    def final_arrive(i, acc):
        source = lax.rem(me_b + N_BEAM - 1 - i, N_BEAM)
        came(fin_in.at[source], fin_send, fin_recv, source).wait_recv()
        return acc + fin_in[source]

    result = lax.fori_loop(0, N_BEAM - 1, final_arrive, fin[me_b])
    out_ref[0] = result[0:2]
    out_ref[1] = result[2:4]

    def sent_ma(i, _):
        peer = lax.rem(me_a + 1 + i, N_MA)
        copy_ma(piece, gathered.at[me_a], ag_send, ag_recv, peer).wait_send()
        copy_ma(gout.at[peer], gin.at[me_a], gr_send, gr_recv, peer).wait_send()
        return 0

    lax.fori_loop(0, N_MA - 1, sent_ma, 0)

    def sent_beam(i, _):
        peer = lax.rem(me_b + 1 + i, N_BEAM)
        copy_beam(partial.at[peer], signals.at[me_b], rs_send, rs_recv, peer).wait_send()
        copy_beam(filtered.at[me_b], filtered.at[me_b], fl_send, fl_recv, peer).wait_send()
        copy_beam(fin.at[peer], fin_in.at[me_b], fin_send, fin_recv, peer).wait_send()
        return 0

    lax.fori_loop(0, N_BEAM - 1, sent_beam, 0)


def local(
    sky_harmonics,
    beam_harmonics,
    wigner,
    order_map,
    block_owner,
    block_local,
    cell_offset,
    cell_fraction,
    beam_angle,
    sample_count,
    noise_weight,
):
    smem = pl.BlockSpec(memory_space=pltpu.SMEM)
    vmem = pl.BlockSpec(memory_space=pltpu.VMEM)
    hbm = pl.BlockSpec(memory_space=pl.ANY)
    dma = pltpu.SemaphoreType.DMA
    owner = block_owner.reshape(NSB)
    return pl.pallas_call(
        kernel,
        out_shape=jax.ShapeDtypeStruct((2, 2, 128), F32),
        in_specs=[smem] * 4 + [vmem] * 2 + [hbm] * 7,
        out_specs=vmem,
        scratch_shapes=[
            pltpu.VMEM((2, 2, 2048), F32),
            pltpu.VMEM((KL, 2, 2048), F32),
            pltpu.VMEM((KL, 2, 64, 2048), BF16),
            pltpu.VMEM((NSB, 128), I32),
            pltpu.VMEM((NSB, 128), F32),
            pltpu.VMEM((NSB, 128), F32),
            pltpu.VMEM((128, 128), F32),
            pltpu.VMEM((128, 128), I32),
            pltpu.VMEM((PHI_BLOCKS, 128, 256), BF16),
            pltpu.VMEM((NSB, KL, 128), F32),
            pltpu.VMEM((NSB, 128, 128), BF16),
            pltpu.VMEM((16, 128), F32),
            pltpu.VMEM((16, 128), BF16),
            pltpu.VMEM((N_MA, 16, 128), BF16),
            pltpu.VMEM((512, 128), F32),
            pltpu.VMEM((64, KL, 128), F32),
            pltpu.VMEM((N_BEAM, 8, 128), F32),
            pltpu.VMEM((N_BEAM, 8, 128), F32),
            pltpu.VMEM((N_BEAM, 8, 128), F32),
            pltpu.VMEM((NSB * KL, 128), F32),
            pltpu.VMEM((512, 128), F32),
            pltpu.VMEM((N_MA, 16, 128), BF16),
            pltpu.VMEM((N_MA, 16, 128), BF16),
            pltpu.VMEM((N_BEAM, 4, 128), F32),
            pltpu.VMEM((N_BEAM, 4, 128), F32),
            dma((6,)),
            dma((4,)),
            dma((N_MA,)),
            dma((N_MA,)),
            dma((N_BEAM,)),
            dma((N_BEAM,)),
            dma((N_BEAM,)),
            dma((N_BEAM,)),
            dma((N_MA,)),
            dma((N_MA,)),
            dma((N_BEAM,)),
            dma((N_BEAM,)),
        ],
        compiler_params=pltpu.CompilerParams(collective_id=0, has_side_effects=True),
        name="normal_operator",
    )(
        owner,
        block_local,
        order_map,
        sample_count,
        owner.reshape(1, NSB),
        block_local.reshape(1, NSB),
        sky_harmonics,
        beam_harmonics,
        wigner,
        cell_offset.reshape(NSB, 128),
        cell_fraction.reshape(NSB, 128),
        beam_angle.reshape(NSB, 128),
        noise_weight,
    )


def solution(mesh):
    return jax.shard_map(
        local,
        mesh=mesh,
        in_specs=(
            P("ma", None, None),
            P("beam", None, None),
            P("beam", "ma", None, None),
            P(),
            P("ma", None),
            P("ma"),
            P("ma"),
            P("ma"),
            P("ma"),
            P("ma"),
            P(),
        ),
        out_specs=P("ma", None, "beam"),
        check_vma=False,
    )
```

```python
import functools
import math

import jax
import jax.numpy as jnp
from jax import lax
from jax.experimental import pallas as pl
from jax.experimental.pallas import tpu as pltpu
from jax.sharding import PartitionSpec as P

F32 = jnp.float32
BF16 = jnp.bfloat16
I32 = jnp.int32

COS_TURNS = (
    0.99999997389483,
    -19.739202931827737,
    64.93907559492132,
    -85.44969773655134,
    60.1656143595228,
    -25.96416606164654,
    6.528151014475474,
)
N_MA = 32
N_BEAM = 16
KL = 8
PHI_BLOCKS = 32
NSB = 128


def cos_turns(turns):
    v = turns - jnp.floor(turns + 0.5)
    w = v * v
    acc = jnp.full_like(w, COS_TURNS[-1])
    for coef in COS_TURNS[-2::-1]:
        acc = acc * w + coef
    return acc


def nn(a, b):
    return lax.dot_general(a, b, (((1,), (0,)), ((), ())), preferred_element_type=F32)


def nt(a, b):
    return lax.dot_general(a, b, (((1,), (1,)), ((), ())), preferred_element_type=F32)


def split(x):
    high = x.astype(BF16)
    return high, (x - high.astype(F32)).astype(BF16)


def kernel(
    owner_hbm,
    local_hbm,
    order_hbm,
    count_s,
    owner_row_hbm,
    local_row_hbm,
    sky_hbm,
    beam_hbm,
    wig_hbm,
    offset_hbm,
    fraction_hbm,
    angle_hbm,
    noise_hbm,
    out_ref,
    owner_s,
    local_s,
    order_s,
    owner_row,
    local_row,
    sky,
    beam,
    wig,
    offset,
    fraction,
    angle,
    noise,
    order,
    phase,
    turn,
    interp,
    rows,
    piece,
    gathered,
    gathered_f,
    modes,
    partial,
    sum_out,
    sum_in,
    sum2_out,
    sum2_in,
    filtered,
    gmat,
    gout_f,
    gpair,
    gout,
    gin,
    fin,
    fin_in,
    load_sem,
    wig_sem,
    ag_send,
    ag_recv,
    agp_send,
    agp_recv,
    s1_send,
    s1_recv,
    s2_send,
    s2_recv,
    grp_send,
    grp_recv,
    gr_send,
    gr_recv,
    fin_send,
    fin_recv,
):
    me_a = lax.axis_index("ma")
    me_b = lax.axis_index("beam")
    z = lax.div(me_a, 2)
    core = lax.rem(me_a, 2)
    x = lax.rem(me_b, 4)
    y = lax.div(me_b, 4)

    loads = [
        pltpu.make_async_copy(src, dst, load_sem.at[i])
        for i, (src, dst) in enumerate(
            [
                (beam_hbm, beam),
                (sky_hbm, sky),
                (order_hbm, order_s),
                (angle_hbm, angle),
                (local_hbm, local_s),
                (owner_hbm, owner_s),
                (offset_hbm, offset),
                (fraction_hbm, fraction),
                (owner_row_hbm, owner_row),
                (local_row_hbm, local_row),
                (noise_hbm, noise),
            ]
        )
    ]
    wig_loads = [
        pltpu.make_async_copy(wig_hbm.at[pl.ds(2 * i, 2)], wig.at[pl.ds(2 * i, 2)], wig_sem.at[i])
        for i in range(4)
    ]
    loads[0].start()
    loads[1].start()
    for copy in wig_loads:
        copy.start()

    barrier = pltpu.get_barrier_semaphore()

    def far_z(i):
        half = (i + 1) // 2
        return lax.rem(z + 16 + 8 + half * (1 - 2 * lax.rem(i, 2)), 16)

    def greet_z(i, _):
        pl.semaphore_signal(barrier, inc=1, device_id={"ma": far_z(i) * 2 + core})
        return 0

    def greet_beam(i, _):
        pl.semaphore_signal(barrier, inc=1, device_id={"beam": lax.rem(me_b + i, N_BEAM)})
        return 0

    partner = z * 2 + 1 - core
    lax.fori_loop(0, 15, greet_z, 0)
    lax.fori_loop(1, N_BEAM, greet_beam, 0)
    pl.semaphore_signal(barrier, inc=1, device_id={"ma": partner})
    for copy in loads[2:]:
        copy.start()

    def remote(src, dst, send, recv, **peer):
        return pltpu.make_async_remote_copy(
            src_ref=src, dst_ref=dst, send_sem=send, recv_sem=recv, device_id=peer
        )

    def to_z(src, dst, send, recv, peer):
        return remote(src, dst, send.at[peer], recv.at[z], ma=peer * 2 + core)

    def to_beam(src, dst, send, recv, peer):
        return remote(src, dst, send.at[peer], recv.at[me_b], beam=peer)

    def came(dst, send, recv):
        return remote(dst, dst, send, recv, ma=me_a)

    loads[0].wait()
    loads[1].wait()
    beam_re = beam[:, 0, :]
    beam_im = beam[:, 1, :]
    products = []
    for m in range(2):
        sky_re = sky[m, 0:1, :]
        sky_im = sky[m, 1:2, :]
        products.append(
            jnp.concatenate(
                [sky_re * beam_re - sky_im * beam_im, sky_re * beam_im + sky_im * beam_re], axis=0
            ).astype(BF16)
        )
    sub = lax.broadcasted_iota(I32, (KL, 128), 0)
    lane = lax.broadcasted_iota(I32, (KL, 128), 1)
    for quad in range(2):
        wig_loads[2 * quad].wait()
        wig_loads[2 * quad + 1].wait()
        for m in range(2):
            weights = jnp.concatenate([wig[4 * quad + k, m] for k in range(4)], axis=0)
            out = nt(products[m], weights)
            for pair in range(2):
                kp = 2 * quad + pair
                keep = sub == 2 * kp + lane // 64
                for c in range(2):
                    part = out[c * KL : (c + 1) * KL, pair * 128 : (pair + 1) * 128]
                    row = (m * 2 + c) * 4 + kp
                    rows[row : row + 1, :] = jnp.sum(
                        jnp.where(keep, part, 0.0), axis=0, keepdims=True
                    )
    piece[...] = rows[...].astype(BF16)

    pl.semaphore_wait(barrier, 15 + 15 + 1)

    def send_modes(i, _):
        to_z(piece, gathered.at[core, z], ag_send, ag_recv, far_z(i)).start()
        return 0

    lax.fori_loop(0, 15, send_modes, 0)
    gathered[core, z] = piece[...]

    for copy in loads[2:]:
        copy.wait()
    for a_core in range(2):
        for a_z in range(16):
            for m in range(2):
                row = (a_core * 16 + a_z) * 4 + m * 2
                order[row : row + 2, :] = jnp.full((2, 128), order_s[(a_z * 2 + a_core) * 2 + m], I32)
    quarter = (lax.broadcasted_iota(I32, (128, 128), 0) % 2).astype(F32) * 0.25

    def phases(b, _):
        cells = (b * 128 + lax.broadcasted_iota(I32, (128, 128), 1)).astype(F32) * (1.0 / 4096.0)
        turns = order[...].astype(F32) * cells + quarter
        high, low = split(cos_turns(turns) * 0.125)
        phase[b] = jnp.concatenate([high, low], axis=1)
        return 0

    lax.fori_loop(0, PHI_BLOCKS, phases, 0)

    beam_order = me_b * KL + sub
    spin = ((beam_order + 1) // 2).astype(F32)
    back = (beam_order % 2).astype(F32) * 0.25

    def turns_of(s, _):
        around = angle[pl.ds(s, 1), :] * (1.0 / (2.0 * math.pi))
        turn[s] = cos_turns(spin * around - back) * (1.0 / math.sqrt(128.0))
        return 0

    lax.fori_loop(0, NSB, turns_of, 0, unroll=4)

    cell = lax.broadcasted_iota(I32, (128, 128), 0)

    def interpolators(s, _):
        block = lax.rem(local_s[s], PHI_BLOCKS)
        low = offset[pl.ds(s, 1), :]
        right = fraction[pl.ds(s, 1), :]
        mix = jnp.where(
            cell == low, 1.0 - right, jnp.where(cell == low + 1, right, 0.0)
        ).astype(BF16)
        interp[s] = nn(phase[block], jnp.concatenate([mix, mix], axis=0)).astype(BF16)
        return 0

    lax.fori_loop(0, NSB, interpolators, 0, unroll=4)

    def modes_arrive(i, _):
        source = far_z(14 - i)
        came(gathered.at[core, source], ag_send.at[source], ag_recv.at[source]).wait_recv()
        return 0

    lax.fori_loop(0, 15, modes_arrive, 0)
    swap_modes = remote(gathered.at[core], gathered.at[core], agp_send, agp_recv, ma=partner)
    swap_modes.start()
    came(gathered.at[1 - core], agp_send, agp_recv).wait_recv()
    gathered_f[...] = gathered[...].astype(F32).reshape(512, 128)
    for kp in range(4):
        block = gathered_f[pl.ds(kp, 128, stride=4), :].T
        modes[:, 2 * kp, :] = block[:64]
        modes[:, 2 * kp + 1, :] = block[64:]

    def forward(first, rows_at):
        for j in range(16):
            s = first + j
            cycle = owner_s[s] * 2 + lax.div(local_s[s], PHI_BLOCKS)
            values = nn(modes[cycle].astype(BF16), interp[s])
            partial[rows_at + j : rows_at + j + 1, :] = jnp.sum(
                turn[s] * values, axis=0, keepdims=True
            )

    def along_x(i):
        return y * 4 + lax.rem(x + i, 4)

    def along_y(i):
        return lax.rem(y + i, 4) * 4 + x

    def exchange(chunk, stage, out, into, send, recv):
        x_first = chunk < 2
        use_x = x_first if stage == 0 else not x_first
        mine = x if use_x else y
        copies = []
        for i in range(1, 4):
            peer = along_x(i) if use_x else along_y(i)
            copies.append(
                remote(
                    out.at[chunk],
                    into.at[chunk, mine],
                    send.at[chunk, i],
                    recv.at[chunk, mine],
                    beam=peer,
                )
            )
        return copies

    def collect(chunk, stage, own, into, send, recv):
        x_first = chunk < 2
        use_x = x_first if stage == 0 else not x_first
        mine = x if use_x else y
        total = own
        for i in range(1, 4):
            source = lax.rem(mine + i, 4)
            came(into.at[chunk, source], send.at[chunk, i], recv.at[chunk, source]).wait_recv()
            total = total + into[chunk, source].astype(F32)
        return total

    first_stage = [exchange(c, 0, sum_out, sum_in, s1_send, s1_recv) for c in range(4)]
    second_stage = [exchange(c, 1, sum2_out, sum2_in, s2_send, s2_recv) for c in range(4)]
    sequence = (0, 2, 1, 3)
    for chunk in sequence:
        forward(chunk * 32, 0)
        forward(chunk * 32 + 16, 16)
        sum_out[chunk] = partial[...].astype(BF16)
        for copy in first_stage[chunk]:
            copy.start()
    for chunk in sequence:
        total = collect(chunk, 0, sum_out[chunk].astype(F32), sum_in, s1_send, s1_recv)
        sum2_out[chunk] = total.astype(BF16)
        for copy in second_stage[chunk]:
            copy.start()

    def backward(first, rows_at):
        for j in range(16):
            s = first + j
            high, low = split(turn[s] * filtered[rows_at + j : rows_at + j + 1, :])
            both = nt(jnp.concatenate([high, low], axis=0), interp[s])
            gmat[s * KL : (s + 1) * KL, :] = both[:KL] + both[KL:]

    for chunk in sequence:
        signal = collect(chunk, 1, sum2_out[chunk].astype(F32), sum2_in, s2_send, s2_recv)
        stamps = (
            chunk * 32 + lax.broadcasted_iota(I32, (32, 128), 0)
        ) * 128 + lax.broadcasted_iota(I32, (32, 128), 1)
        valid = (stamps < count_s[0]).astype(F32)
        filtered[...] = (
            lax.dot_general(
                signal * valid,
                noise[...],
                (((1,), (1,)), ((), ())),
                precision=lax.Precision.HIGHEST,
                preferred_element_type=F32,
            )
            * valid
        )
        backward(chunk * 32, 0)
        backward(chunk * 32 + 16, 16)

    cycles = owner_row[...] * 2 + lax.div(local_row[...], jnp.full((1, NSB), PHI_BLOCKS, I32))
    pick = (lax.broadcasted_iota(I32, (64, 128), 0) == cycles).astype(F32).astype(BF16)
    pick = jnp.concatenate([pick, pick], axis=1)
    for kp in range(4):
        halves = []
        for k in (2 * kp, 2 * kp + 1):
            high, low = split(gmat[pl.ds(k, 128, stride=KL), :])
            halves.append(nn(pick, jnp.concatenate([high, low], axis=0)))
        gout_f[pl.ds(kp, 128, stride=4), :] = jnp.concatenate(halves, axis=0).T

    half_rows = pl.multiple_of(core * 256, 256)
    other_rows = pl.multiple_of((1 - core) * 256, 256)
    swap_grads = remote(gout_f.at[pl.ds(other_rows, 256)], gpair, grp_send, grp_recv, ma=partner)
    swap_grads.start()
    swap_modes.wait_send()

    def sent_modes(i, _):
        peer = far_z(i)
        to_z(piece, gathered.at[core, z], ag_send, ag_recv, peer).wait_send()
        return 0

    lax.fori_loop(0, 15, sent_modes, 0)
    came(gpair, grp_send, grp_recv).wait_recv()
    gout[...] = (gout_f[pl.ds(half_rows, 256), :] + gpair[...]).reshape(16, 16, 128).astype(BF16)

    def send_grads(i, _):
        peer = far_z(i)
        to_z(gout.at[peer], gin.at[z], gr_send, gr_recv, peer).start()
        return 0

    lax.fori_loop(0, 15, send_grads, 0)
    for chunk in range(4):
        for copy in first_stage[chunk] + second_stage[chunk]:
            copy.wait_send()
    swap_grads.wait_send()

    def grads_arrive(i, acc):
        source = far_z(14 - i)
        came(gin.at[source], gr_send.at[source], gr_recv.at[source]).wait_recv()
        return acc + gin[source].astype(F32)

    rows[...] = lax.fori_loop(0, 15, grads_arrive, gout[z].astype(F32))

    for m in range(2):
        lhs = []
        for c in range(2):
            for kp in range(4):
                row = (m * 2 + c) * 4 + kp
                spreadout = jnp.broadcast_to(rows[row : row + 1, :], (KL, 128))
                lhs.append(jnp.where(sub == 2 * kp + lane // 64, spreadout, 0.0))
        lhs = jnp.concatenate(
            [jnp.concatenate(lhs[:4], axis=1), jnp.concatenate(lhs[4:], axis=1)], axis=0
        ).astype(BF16)
        weights = jnp.concatenate([wig[k, m] for k in range(KL)], axis=0)
        harm = nn(lhs, weights)
        re, im = harm[:KL], harm[KL:]
        first = jnp.sum(re * beam_re + im * beam_im, axis=0, keepdims=True)
        second = jnp.sum(im * beam_re - re * beam_im, axis=0, keepdims=True)
        for b in range(N_BEAM):
            fin[b, 2 * m : 2 * m + 1, :] = first[:, b * 128 : (b + 1) * 128]
            fin[b, 2 * m + 1 : 2 * m + 2, :] = second[:, b * 128 : (b + 1) * 128]

    def send_final(i, _):
        peer = lax.rem(me_b + 1 + i, N_BEAM)
        to_beam(fin.at[peer], fin_in.at[me_b], fin_send, fin_recv, peer).start()
        return 0

    lax.fori_loop(0, N_BEAM - 1, send_final, 0)

    def sent_grads(i, _):
        peer = far_z(i)
        to_z(gout.at[peer], gin.at[z], gr_send, gr_recv, peer).wait_send()
        return 0

    lax.fori_loop(0, 15, sent_grads, 0)

    def final_arrive(i, acc):
        source = lax.rem(me_b + N_BEAM - 1 - i, N_BEAM)
        came(fin_in.at[source], fin_send.at[source], fin_recv.at[source]).wait_recv()
        return acc + fin_in[source]

    result = lax.fori_loop(0, N_BEAM - 1, final_arrive, fin[me_b])
    out_ref[0] = result[0:2]
    out_ref[1] = result[2:4]

    def sent_final(i, _):
        peer = lax.rem(me_b + 1 + i, N_BEAM)
        to_beam(fin.at[peer], fin_in.at[me_b], fin_send, fin_recv, peer).wait_send()
        return 0

    lax.fori_loop(0, N_BEAM - 1, sent_final, 0)


def local(
    sky_harmonics,
    beam_harmonics,
    wigner,
    order_map,
    block_owner,
    block_local,
    cell_offset,
    cell_fraction,
    beam_angle,
    sample_count,
    noise_weight,
):
    hbm = pl.BlockSpec(memory_space=pl.ANY)
    vmem, smem, dma = pltpu.VMEM, pltpu.SMEM, pltpu.SemaphoreType.DMA
    owner = block_owner.reshape(NSB)
    return pl.pallas_call(
        kernel,
        out_shape=jax.ShapeDtypeStruct((2, 2, 128), F32),
        in_specs=[hbm] * 3 + [pl.BlockSpec(memory_space=smem)] + [hbm] * 9,
        out_specs=pl.BlockSpec(memory_space=pltpu.VMEM),
        scratch_shapes=[
            smem((NSB,), I32),
            smem((NSB,), I32),
            smem((64,), I32),
            vmem((1, NSB), I32),
            vmem((1, NSB), I32),
            vmem((2, 2, 2048), F32),
            vmem((KL, 2, 2048), F32),
            vmem((KL, 2, 64, 2048), BF16),
            vmem((NSB, 128), I32),
            vmem((NSB, 128), F32),
            vmem((NSB, 128), F32),
            vmem((128, 128), F32),
            vmem((128, 128), I32),
            vmem((PHI_BLOCKS, 128, 256), BF16),
            vmem((NSB, KL, 128), F32),
            vmem((NSB, 128, 128), BF16),
            vmem((16, 128), F32),
            vmem((16, 128), BF16),
            vmem((2, 16, 16, 128), BF16),
            vmem((512, 128), F32),
            vmem((64, KL, 128), F32),
            vmem((32, 128), F32),
            vmem((4, 32, 128), BF16),
            vmem((4, 4, 32, 128), BF16),
            vmem((4, 32, 128), BF16),
            vmem((4, 4, 32, 128), BF16),
            vmem((32, 128), F32),
            vmem((NSB * KL, 128), F32),
            vmem((512, 128), F32),
            vmem((256, 128), F32),
            vmem((16, 16, 128), BF16),
            vmem((16, 16, 128), BF16),
            vmem((N_BEAM, 4, 128), F32),
            vmem((N_BEAM, 4, 128), F32),
            dma((11,)),
            dma((4,)),
            dma((16,)),
            dma((16,)),
            dma,
            dma,
            dma((4, 4)),
            dma((4, 4)),
            dma((4, 4)),
            dma((4, 4)),
            dma,
            dma,
            dma((16,)),
            dma((16,)),
            dma((N_BEAM,)),
            dma((N_BEAM,)),
        ],
        compiler_params=pltpu.CompilerParams(collective_id=0, has_side_effects=True),
        name="normal_operator",
    )(
        owner,
        block_local,
        order_map,
        sample_count,
        owner.reshape(1, NSB),
        block_local.reshape(1, NSB),
        sky_harmonics,
        beam_harmonics,
        wigner,
        cell_offset.reshape(NSB, 128),
        cell_fraction.reshape(NSB, 128),
        beam_angle.reshape(NSB, 128),
        noise_weight,
    )


def solution(mesh):
    return jax.shard_map(
        local,
        mesh=mesh,
        in_specs=(
            P("ma", None, None),
            P("beam", None, None),
            P("beam", "ma", None, None),
            P(),
            P("ma", None),
            P("ma"),
            P("ma"),
            P("ma"),
            P("ma"),
            P("ma"),
            P(),
        ),
        out_specs=P("ma", None, "beam"),
        check_vma=False,
    )
```

```python
import functools
import math

import jax
import jax.numpy as jnp
from jax import lax
from jax.experimental import pallas as pl
from jax.experimental.pallas import tpu as pltpu
from jax.sharding import PartitionSpec as P

F32 = jnp.float32
BF16 = jnp.bfloat16
I32 = jnp.int32

COS_TURNS = (
    0.99999997389483,
    -19.739202931827737,
    64.93907559492132,
    -85.44969773655134,
    60.1656143595228,
    -25.96416606164654,
    6.528151014475474,
)
N_MA = 32
N_BEAM = 16
KL = 8
PHI_BLOCKS = 32
NSB = 128
EARLY = 16


def cos_turns(turns):
    v = turns - jnp.floor(turns + 0.5)
    w = v * v
    acc = jnp.full_like(w, COS_TURNS[-1])
    for coef in COS_TURNS[-2::-1]:
        acc = acc * w + coef
    return acc


def nn(a, b):
    return lax.dot_general(a, b, (((1,), (0,)), ((), ())), preferred_element_type=F32)


def nt(a, b):
    return lax.dot_general(a, b, (((1,), (1,)), ((), ())), preferred_element_type=F32)


def split(x):
    high = x.astype(BF16)
    return high, (x - high.astype(F32)).astype(BF16)


def kernel(
    owner_hbm,
    local_hbm,
    order_hbm,
    count_s,
    owner_row_hbm,
    local_row_hbm,
    sky_hbm,
    beam_hbm,
    wig_hbm,
    offset_hbm,
    fraction_hbm,
    angle_hbm,
    noise_hbm,
    out_ref,
    owner_s,
    local_s,
    order_s,
    owner_row,
    local_row,
    sky,
    beam,
    wig,
    offset,
    fraction,
    angle,
    noise,
    order,
    phase,
    turn,
    interp,
    rows,
    piece,
    gathered,
    gathered_f,
    modes,
    partial,
    sum_out,
    sum_in,
    sum2_out,
    sum2_in,
    filtered,
    gmat,
    gout_f,
    gpair,
    gout,
    gin,
    fin,
    fin_in,
    load_sem,
    wig_sem,
    ag_send,
    ag_recv,
    agp_send,
    agp_recv,
    s1_send,
    s1_recv,
    s2_send,
    s2_recv,
    grp_send,
    grp_recv,
    gr_send,
    gr_recv,
    fin_send,
    fin_recv,
):
    me_a = lax.axis_index("ma")
    me_b = lax.axis_index("beam")
    z = lax.div(me_a, 2)
    core = lax.rem(me_a, 2)
    x = lax.rem(me_b, 4)
    y = lax.div(me_b, 4)

    loads = [
        pltpu.make_async_copy(src, dst, load_sem.at[i])
        for i, (src, dst) in enumerate(
            [
                (beam_hbm, beam),
                (sky_hbm, sky),
                (order_hbm, order_s),
                (angle_hbm, angle),
                (local_hbm, local_s),
                (owner_hbm, owner_s),
                (offset_hbm, offset),
                (fraction_hbm, fraction),
                (owner_row_hbm, owner_row),
                (local_row_hbm, local_row),
                (noise_hbm, noise),
            ]
        )
    ]
    wig_loads = [
        pltpu.make_async_copy(wig_hbm.at[pl.ds(2 * i, 2)], wig.at[pl.ds(2 * i, 2)], wig_sem.at[i])
        for i in range(4)
    ]
    loads[0].start()
    loads[1].start()
    for copy in wig_loads:
        copy.start()

    barrier = pltpu.get_barrier_semaphore()

    def far_z(i):
        half = (i + 1) // 2
        return lax.rem(z + 16 + 8 + half * (1 - 2 * lax.rem(i, 2)), 16)

    def along_x(i):
        return y * 4 + lax.rem(x + i, 4)

    def along_y(i):
        return lax.rem(y + i, 4) * 4 + x

    def on_z(distance):
        return lax.rem(z + 16 + distance, 16)

    near = (4, -4, 3, -3, 2, -2, 1, -1)
    partner = z * 2 + 1 - core
    for distance in near:
        pl.semaphore_signal(barrier, inc=1, device_id={"ma": on_z(distance) * 2 + core})
    for i in (2, 1, 3):
        pl.semaphore_signal(barrier, inc=1, device_id={"beam": along_x(i)})
        pl.semaphore_signal(barrier, inc=1, device_id={"beam": along_y(i)})
    pl.semaphore_signal(barrier, inc=1, device_id={"ma": partner})
    for copy in loads[2:]:
        copy.start()

    def remote(src, dst, send, recv, **peer):
        return pltpu.make_async_remote_copy(
            src_ref=src, dst_ref=dst, send_sem=send, recv_sem=recv, device_id=peer
        )

    def to_z(src, dst, send, recv, peer):
        return remote(src, dst, send.at[peer], recv.at[z], ma=peer * 2 + core)

    def to_beam(src, dst, send, recv, peer):
        return remote(src, dst, send.at[peer], recv.at[me_b], beam=peer)

    def came(dst, send, recv):
        return remote(dst, dst, send, recv, ma=me_a)

    loads[0].wait()
    loads[1].wait()
    beam_re = beam[:, 0, :]
    beam_im = beam[:, 1, :]
    products = []
    for m in range(2):
        sky_re = sky[m, 0:1, :]
        sky_im = sky[m, 1:2, :]
        products.append(
            jnp.concatenate(
                [sky_re * beam_re - sky_im * beam_im, sky_re * beam_im + sky_im * beam_re], axis=0
            ).astype(BF16)
        )
    sub = lax.broadcasted_iota(I32, (KL, 128), 0)
    lane = lax.broadcasted_iota(I32, (KL, 128), 1)
    for quad in range(2):
        wig_loads[2 * quad].wait()
        wig_loads[2 * quad + 1].wait()
        for m in range(2):
            weights = jnp.concatenate([wig[4 * quad + k, m] for k in range(4)], axis=0)
            out = nt(products[m], weights)
            for pair in range(2):
                kp = 2 * quad + pair
                keep = sub == 2 * kp + lane // 64
                for c in range(2):
                    part = out[c * KL : (c + 1) * KL, pair * 128 : (pair + 1) * 128]
                    row = (m * 2 + c) * 4 + kp
                    rows[row : row + 1, :] = jnp.sum(
                        jnp.where(keep, part, 0.0), axis=0, keepdims=True
                    )
    piece[...] = rows[...].astype(BF16)

    pl.semaphore_wait(barrier, len(near) + 6 + 1)
    sent_modes = []
    for i, distance in enumerate(near):
        sent_modes.append(
            remote(
                piece,
                gathered.at[core, z],
                ag_send.at[i],
                ag_recv.at[z],
                ma=on_z(distance) * 2 + core,
            )
        )
        sent_modes[-1].start()
    gathered[core, z] = piece[...]

    for copy in loads[2:]:
        copy.wait()
    for a_core in range(2):
        for a_z in range(16):
            for m in range(2):
                row = (a_core * 16 + a_z) * 4 + m * 2
                order[row : row + 2, :] = jnp.full((2, 128), order_s[(a_z * 2 + a_core) * 2 + m], I32)
    quarter = (lax.broadcasted_iota(I32, (128, 128), 0) % 2).astype(F32) * 0.25

    def phases(b, _):
        cells = (b * 128 + lax.broadcasted_iota(I32, (128, 128), 1)).astype(F32) * (1.0 / 4096.0)
        turns = order[...].astype(F32) * cells + quarter
        high, low = split(cos_turns(turns) * 0.125)
        phase[b] = jnp.concatenate([high, low], axis=1)
        return 0

    lax.fori_loop(0, PHI_BLOCKS, phases, 0)

    beam_order = me_b * KL + sub
    spin = ((beam_order + 1) // 2).astype(F32)
    back = (beam_order % 2).astype(F32) * 0.25

    def turns_of(s, _):
        around = angle[pl.ds(s, 1), :] * (1.0 / (2.0 * math.pi))
        turn[s] = cos_turns(spin * around - back) * (1.0 / math.sqrt(128.0))
        return 0

    lax.fori_loop(0, NSB, turns_of, 0, unroll=4)

    cell = lax.broadcasted_iota(I32, (128, 128), 0)

    def interpolator(s):
        block = lax.rem(local_s[s], PHI_BLOCKS)
        low = offset[pl.ds(s, 1), :]
        right = fraction[pl.ds(s, 1), :]
        mix = jnp.where(
            cell == low, 1.0 - right, jnp.where(cell == low + 1, right, 0.0)
        ).astype(BF16)
        return nn(phase[block], jnp.concatenate([mix, mix], axis=0)).astype(BF16)

    def interpolator_pair(i, _):
        interp[i] = jnp.concatenate([interpolator(2 * i), interpolator(2 * i + 1)], axis=1)
        return 0

    def modes_of(distance):
        source = on_z(distance)
        came(gathered.at[core, source], ag_send.at[0], ag_recv.at[source]).wait_recv()

    lax.fori_loop(0, EARLY, interpolator_pair, 0, unroll=2)

    for source, onward in ((-4, (4, 3, 2, 1)), (4, (-3, -2, -1))):
        modes_of(source)
        block = gathered.at[core, on_z(source)]
        for distance in onward:
            i = len(sent_modes)
            sent_modes.append(
                remote(
                    block,
                    block,
                    ag_send.at[i],
                    ag_recv.at[on_z(source)],
                    ma=on_z(distance) * 2 + core,
                )
            )
            sent_modes[-1].start()
    lax.fori_loop(EARLY, NSB // 2, interpolator_pair, 0, unroll=2)
    for distance in (3, -3, 2, -2, 1, -1, 5, -5, 6, -6, 7, -7, 8):
        modes_of(distance)
    swap_modes = remote(gathered.at[core], gathered.at[core], agp_send, agp_recv, ma=partner)
    swap_modes.start()
    came(gathered.at[1 - core], agp_send, agp_recv).wait_recv()
    gathered_f[...] = gathered[...].astype(F32).reshape(512, 128)
    for kp in range(4):
        block = gathered_f[pl.ds(kp, 128, stride=4), :].T
        modes[:, 2 * kp, :] = block[:64]
        modes[:, 2 * kp + 1, :] = block[64:]

    def forward(first, rows_at):
        for j in range(0, 16, 2):
            own = []
            for s in (first + j, first + j + 1):
                own.append(modes[owner_s[s] * 2 + lax.div(local_s[s], PHI_BLOCKS)])
            values = nn(jnp.concatenate(own, axis=0).astype(BF16), interp[(first + j) // 2])
            for i in range(2):
                part = values[i * KL : (i + 1) * KL, i * 128 : (i + 1) * 128]
                partial[rows_at + j + i : rows_at + j + i + 1, :] = jnp.sum(
                    turn[first + j + i] * part, axis=0, keepdims=True
                )

    def exchange(chunk, stage, out, into, send, recv):
        x_first = chunk < 2
        use_x = x_first if stage == 0 else not x_first
        mine = x if use_x else y
        copies = []
        for i in range(1, 4):
            peer = along_x(i) if use_x else along_y(i)
            copies.append(
                remote(
                    out.at[chunk],
                    into.at[chunk, mine],
                    send.at[chunk, i],
                    recv.at[chunk, mine],
                    beam=peer,
                )
            )
        return copies

    def collect(chunk, stage, own, into, send, recv):
        x_first = chunk < 2
        use_x = x_first if stage == 0 else not x_first
        mine = x if use_x else y
        total = own
        for i in range(1, 4):
            source = lax.rem(mine + i, 4)
            came(into.at[chunk, source], send.at[chunk, i], recv.at[chunk, source]).wait_recv()
            total = total + into[chunk, source].astype(F32)
        return total

    first_stage = [exchange(c, 0, sum_out, sum_in, s1_send, s1_recv) for c in range(4)]
    second_stage = [exchange(c, 1, sum2_out, sum2_in, s2_send, s2_recv) for c in range(4)]
    sequence = (0, 2, 1, 3)
    for chunk in sequence:
        forward(chunk * 32, 0)
        forward(chunk * 32 + 16, 16)
        sum_out[chunk] = partial[...].astype(BF16)
        for copy in first_stage[chunk]:
            copy.start()
    for chunk in sequence:
        total = collect(chunk, 0, sum_out[chunk].astype(F32), sum_in, s1_send, s1_recv)
        sum2_out[chunk] = total.astype(BF16)
        for copy in second_stage[chunk]:
            copy.start()

    def backward(first, rows_at):
        for j in range(0, 16, 2):
            lhs = []
            for i in (j, j + 1):
                lhs += split(turn[first + i] * filtered[rows_at + i : rows_at + i + 1, :])
            weights = interp[(first + j) // 2]
            weights = jnp.concatenate([weights[:, :128], weights[:, 128:]], axis=0)
            both = nt(jnp.concatenate(lhs, axis=0), weights)
            s = first + j
            gmat[s * KL : (s + 1) * KL, :] = both[:KL, :128] + both[KL : 2 * KL, :128]
            gmat[(s + 1) * KL : (s + 2) * KL, :] = (
                both[2 * KL : 3 * KL, 128:] + both[3 * KL :, 128:]
            )

    for chunk in sequence:
        signal = collect(chunk, 1, sum2_out[chunk].astype(F32), sum2_in, s2_send, s2_recv)
        stamps = (
            chunk * 32 + lax.broadcasted_iota(I32, (32, 128), 0)
        ) * 128 + lax.broadcasted_iota(I32, (32, 128), 1)
        valid = (stamps < count_s[0]).astype(F32)
        filtered[...] = (
            lax.dot_general(
                signal * valid,
                noise[...],
                (((1,), (1,)), ((), ())),
                precision=lax.Precision.HIGHEST,
                preferred_element_type=F32,
            )
            * valid
        )
        backward(chunk * 32, 0)
        backward(chunk * 32 + 16, 16)

    cycles = owner_row[...] * 2 + lax.div(local_row[...], jnp.full((1, NSB), PHI_BLOCKS, I32))
    pick = (lax.broadcasted_iota(I32, (64, 128), 0) == cycles).astype(F32).astype(BF16)
    pick = jnp.concatenate([pick, pick], axis=1)
    for kp in range(4):
        halves = []
        for k in (2 * kp, 2 * kp + 1):
            high, low = split(gmat[pl.ds(k, 128, stride=KL), :])
            halves.append(nn(pick, jnp.concatenate([high, low], axis=0)))
        gout_f[pl.ds(kp, 128, stride=4), :] = jnp.concatenate(halves, axis=0).T

    half_rows = pl.multiple_of(core * 256, 256)
    other_rows = pl.multiple_of((1 - core) * 256, 256)
    swap_grads = remote(gout_f.at[pl.ds(other_rows, 256)], gpair, grp_send, grp_recv, ma=partner)
    swap_grads.start()
    swap_modes.wait_send()
    for copy in sent_modes:
        copy.wait_send()
    came(gpair, grp_send, grp_recv).wait_recv()
    gout[...] = (gout_f[pl.ds(half_rows, 256), :] + gpair[...]).reshape(16, 16, 128).astype(BF16)

    def send_grads(i, _):
        peer = far_z(i)
        to_z(gout.at[peer], gin.at[z], gr_send, gr_recv, peer).start()
        return 0

    lax.fori_loop(0, 15, send_grads, 0)
    for chunk in range(4):
        for copy in first_stage[chunk] + second_stage[chunk]:
            copy.wait_send()
    swap_grads.wait_send()

    def grads_arrive(i, acc):
        source = far_z(14 - i)
        came(gin.at[source], gr_send.at[source], gr_recv.at[source]).wait_recv()
        return acc + gin[source].astype(F32)

    rows[...] = lax.fori_loop(0, 15, grads_arrive, gout[z].astype(F32))

    for m in range(2):
        lhs = []
        for c in range(2):
            for kp in range(4):
                row = (m * 2 + c) * 4 + kp
                spreadout = jnp.broadcast_to(rows[row : row + 1, :], (KL, 128))
                lhs.append(jnp.where(sub == 2 * kp + lane // 64, spreadout, 0.0))
        lhs = jnp.concatenate(
            [jnp.concatenate(lhs[:4], axis=1), jnp.concatenate(lhs[4:], axis=1)], axis=0
        ).astype(BF16)
        weights = jnp.concatenate([wig[k, m] for k in range(KL)], axis=0)
        harm = nn(lhs, weights)
        re, im = harm[:KL], harm[KL:]
        first = jnp.sum(re * beam_re + im * beam_im, axis=0, keepdims=True)
        second = jnp.sum(im * beam_re - re * beam_im, axis=0, keepdims=True)
        for b in range(N_BEAM):
            fin[b, 2 * m : 2 * m + 1, :] = first[:, b * 128 : (b + 1) * 128]
            fin[b, 2 * m + 1 : 2 * m + 2, :] = second[:, b * 128 : (b + 1) * 128]

    def send_final(i, _):
        peer = lax.rem(me_b + 1 + i, N_BEAM)
        to_beam(fin.at[peer], fin_in.at[me_b], fin_send, fin_recv, peer).start()
        return 0

    lax.fori_loop(0, N_BEAM - 1, send_final, 0)

    def sent_grads(i, _):
        peer = far_z(i)
        to_z(gout.at[peer], gin.at[z], gr_send, gr_recv, peer).wait_send()
        return 0

    lax.fori_loop(0, 15, sent_grads, 0)

    def final_arrive(i, acc):
        source = lax.rem(me_b + N_BEAM - 1 - i, N_BEAM)
        came(fin_in.at[source], fin_send.at[source], fin_recv.at[source]).wait_recv()
        return acc + fin_in[source]

    result = lax.fori_loop(0, N_BEAM - 1, final_arrive, fin[me_b])
    out_ref[0] = result[0:2]
    out_ref[1] = result[2:4]

    def sent_final(i, _):
        peer = lax.rem(me_b + 1 + i, N_BEAM)
        to_beam(fin.at[peer], fin_in.at[me_b], fin_send, fin_recv, peer).wait_send()
        return 0

    lax.fori_loop(0, N_BEAM - 1, sent_final, 0)


def local(
    sky_harmonics,
    beam_harmonics,
    wigner,
    order_map,
    block_owner,
    block_local,
    cell_offset,
    cell_fraction,
    beam_angle,
    sample_count,
    noise_weight,
):
    hbm = pl.BlockSpec(memory_space=pl.ANY)
    vmem, smem, dma = pltpu.VMEM, pltpu.SMEM, pltpu.SemaphoreType.DMA
    owner = block_owner.reshape(NSB)
    return pl.pallas_call(
        kernel,
        out_shape=pltpu.VMEM((2, 2, 128), F32),
        in_specs=[hbm] * 3 + [pl.BlockSpec(memory_space=smem)] + [hbm] * 9,
        out_specs=pl.BlockSpec(memory_space=pltpu.VMEM),
        scratch_shapes=[
            smem((NSB,), I32),
            smem((NSB,), I32),
            smem((64,), I32),
            vmem((1, NSB), I32),
            vmem((1, NSB), I32),
            vmem((2, 2, 2048), F32),
            vmem((KL, 2, 2048), F32),
            vmem((KL, 2, 64, 2048), BF16),
            vmem((NSB, 128), I32),
            vmem((NSB, 128), F32),
            vmem((NSB, 128), F32),
            vmem((128, 128), F32),
            vmem((128, 128), I32),
            vmem((PHI_BLOCKS, 128, 256), BF16),
            vmem((NSB, KL, 128), F32),
            vmem((NSB // 2, 128, 256), BF16),
            vmem((16, 128), F32),
            vmem((16, 128), BF16),
            vmem((2, 16, 16, 128), BF16),
            vmem((512, 128), F32),
            vmem((64, KL, 128), F32),
            vmem((32, 128), F32),
            vmem((4, 32, 128), BF16),
            vmem((4, 4, 32, 128), BF16),
            vmem((4, 32, 128), BF16),
            vmem((4, 4, 32, 128), BF16),
            vmem((32, 128), F32),
            vmem((NSB * KL, 128), F32),
            vmem((512, 128), F32),
            vmem((256, 128), F32),
            vmem((16, 16, 128), BF16),
            vmem((16, 16, 128), BF16),
            vmem((N_BEAM, 4, 128), F32),
            vmem((N_BEAM, 4, 128), F32),
            dma((11,)),
            dma((4,)),
            dma((16,)),
            dma((16,)),
            dma,
            dma,
            dma((4, 4)),
            dma((4, 4)),
            dma((4, 4)),
            dma((4, 4)),
            dma,
            dma,
            dma((16,)),
            dma((16,)),
            dma((N_BEAM,)),
            dma((N_BEAM,)),
        ],
        compiler_params=pltpu.CompilerParams(collective_id=0, has_side_effects=True),
        name="normal_operator",
    )(
        owner,
        block_local,
        order_map,
        sample_count,
        owner.reshape(1, NSB),
        block_local.reshape(1, NSB),
        sky_harmonics,
        beam_harmonics,
        wigner,
        cell_offset.reshape(NSB, 128),
        cell_fraction.reshape(NSB, 128),
        beam_angle.reshape(NSB, 128),
        noise_weight,
    )


def solution(mesh):
    return jax.shard_map(
        local,
        mesh=mesh,
        in_specs=(
            P("ma", None, None),
            P("beam", None, None),
            P("beam", "ma", None, None),
            P(),
            P("ma", None),
            P("ma"),
            P("ma"),
            P("ma"),
            P("ma"),
            P("ma"),
            P(),
        ),
        out_specs=P("ma", None, "beam"),
        check_vma=False,
    )
```

```python
import functools
import math

import jax
import jax.numpy as jnp
from jax import lax
from jax.experimental import pallas as pl
from jax.experimental.pallas import tpu as pltpu
from jax.sharding import PartitionSpec as P

F32 = jnp.float32
BF16 = jnp.bfloat16
I32 = jnp.int32

COS_TURNS = (
    0.99999997389483,
    -19.739202931827737,
    64.93907559492132,
    -85.44969773655134,
    60.1656143595228,
    -25.96416606164654,
    6.528151014475474,
)
N_MA = 32
N_BEAM = 16
KL = 8
PHI_BLOCKS = 32
NSB = 128
EARLY = 16


def cos_turns(turns):
    v = turns - jnp.floor(turns + 0.5)
    w = v * v
    acc = jnp.full_like(w, COS_TURNS[-1])
    for coef in COS_TURNS[-2::-1]:
        acc = acc * w + coef
    return acc


def nn(a, b):
    return lax.dot_general(a, b, (((1,), (0,)), ((), ())), preferred_element_type=F32)


def nt(a, b):
    return lax.dot_general(a, b, (((1,), (1,)), ((), ())), preferred_element_type=F32)


def split(x):
    high = x.astype(BF16)
    return high, (x - high.astype(F32)).astype(BF16)


def kernel(
    owner_hbm,
    local_hbm,
    order_hbm,
    count_s,
    owner_row_hbm,
    local_row_hbm,
    sky_hbm,
    beam_hbm,
    wig_hbm,
    offset_hbm,
    fraction_hbm,
    angle_hbm,
    noise_hbm,
    out_ref,
    owner_s,
    local_s,
    order_s,
    owner_row,
    local_row,
    sky,
    beam,
    wig,
    offset,
    fraction,
    angle,
    noise,
    order,
    phase,
    turn,
    interp,
    rows,
    piece,
    gathered,
    gathered_f,
    modes,
    partial,
    sum_out,
    sum_in,
    sum2_out,
    sum2_in,
    filtered,
    gmat,
    gout_f,
    gpair,
    gout,
    gin,
    fin,
    fin_in,
    load_sem,
    wig_sem,
    ag_send,
    ag_recv,
    agp_send,
    agp_recv,
    s1_send,
    s1_recv,
    s2_send,
    s2_recv,
    grp_send,
    grp_recv,
    gr_send,
    gr_recv,
    fin_send,
    fin_recv,
):
    me_a = lax.axis_index("ma")
    me_b = lax.axis_index("beam")
    z = lax.div(me_a, 2)
    core = lax.rem(me_a, 2)
    x = lax.rem(me_b, 4)
    y = lax.div(me_b, 4)

    loads = [
        pltpu.make_async_copy(src, dst, load_sem.at[i])
        for i, (src, dst) in enumerate(
            [
                (order_hbm, order_s),
                (angle_hbm, angle),
                (beam_hbm, beam),
                (sky_hbm, sky),
                (local_hbm, local_s),
                (owner_hbm, owner_s),
                (offset_hbm, offset),
                (fraction_hbm, fraction),
                (owner_row_hbm, owner_row),
                (local_row_hbm, local_row),
                (noise_hbm, noise),
            ]
        )
    ]
    wig_loads = [
        pltpu.make_async_copy(wig_hbm.at[pl.ds(2 * i, 2)], wig.at[pl.ds(2 * i, 2)], wig_sem.at[i])
        for i in range(4)
    ]
    for copy in loads[:4] + wig_loads + loads[4:]:
        copy.start()

    barrier = pltpu.get_barrier_semaphore()

    def far_z(i):
        half = (i + 1) // 2
        return lax.rem(z + 16 + 8 + half * (1 - 2 * lax.rem(i, 2)), 16)

    def along_x(i):
        return y * 4 + lax.rem(x + i, 4)

    def along_y(i):
        return lax.rem(y + i, 4) * 4 + x

    def on_z(distance):
        return lax.rem(z + 16 + distance, 16)

    near = (4, -4, 3, -3, 2, -2, 1, -1)
    partner = z * 2 + 1 - core
    for distance in near:
        pl.semaphore_signal(barrier, inc=1, device_id={"ma": on_z(distance) * 2 + core})
    for i in (2, 1, 3):
        pl.semaphore_signal(barrier, inc=1, device_id={"beam": along_x(i)})
        pl.semaphore_signal(barrier, inc=1, device_id={"beam": along_y(i)})
    pl.semaphore_signal(barrier, inc=1, device_id={"ma": partner})

    def remote(src, dst, send, recv, **peer):
        return pltpu.make_async_remote_copy(
            src_ref=src, dst_ref=dst, send_sem=send, recv_sem=recv, device_id=peer
        )

    def to_z(src, dst, send, recv, peer):
        return remote(src, dst, send.at[peer], recv.at[z], ma=peer * 2 + core)

    def to_beam(src, dst, send, recv, peer):
        return remote(src, dst, send.at[peer], recv.at[me_b], beam=peer)

    def came(dst, send, recv):
        return remote(dst, dst, send, recv, ma=me_a)

    sub = lax.broadcasted_iota(I32, (KL, 128), 0)
    lane = lax.broadcasted_iota(I32, (KL, 128), 1)

    loads[0].wait()
    for a_core in range(2):
        for a_z in range(16):
            for m in range(2):
                row = (a_core * 16 + a_z) * 4 + m * 2
                order[row : row + 2, :] = jnp.full((2, 128), order_s[(a_z * 2 + a_core) * 2 + m], I32)
    for half in range(2):
        orders = order[half * 64 : half * 64 + 64, :].astype(F32)
        cells = lax.broadcasted_iota(I32, (64, 128), 1).astype(F32) * (1.0 / 4096.0)
        quarter = (lax.broadcasted_iota(I32, (64, 128), 0) % 2).astype(F32) * 0.25
        start = orders * cells + quarter
        step = orders * (1.0 / 32.0)
        step_re = cos_turns(step)
        step_im = cos_turns(step - 0.25)

        def phases(b, carried):
            re, im = carried
            phase[b, half * 64 : half * 64 + 64, :] = re.astype(BF16)
            return re * step_re - im * step_im, im * step_re + re * step_im

        lax.fori_loop(
            0,
            PHI_BLOCKS,
            phases,
            (cos_turns(start) * 0.125, cos_turns(start - 0.25) * 0.125),
            unroll=2,
        )
    loads[1].wait()
    beam_order = me_b * KL + sub
    spin = ((beam_order + 1) // 2).astype(F32)
    back = (beam_order % 2).astype(F32) * 0.25

    def turns_of(s, _):
        around = angle[pl.ds(s, 1), :] * (1.0 / (2.0 * math.pi))
        turn[s] = cos_turns(spin * around - back) * (1.0 / math.sqrt(128.0))
        return 0

    lax.fori_loop(0, NSB, turns_of, 0, unroll=4)

    loads[2].wait()
    loads[3].wait()
    beam_re = beam[:, 0, :]
    beam_im = beam[:, 1, :]
    products = []
    for m in range(2):
        sky_re = sky[m, 0:1, :]
        sky_im = sky[m, 1:2, :]
        products.append(
            jnp.concatenate(
                [sky_re * beam_re - sky_im * beam_im, sky_re * beam_im + sky_im * beam_re], axis=0
            ).astype(BF16)
        )
    for quad in range(2):
        wig_loads[2 * quad].wait()
        wig_loads[2 * quad + 1].wait()
        for m in range(2):
            weights = jnp.concatenate([wig[4 * quad + k, m] for k in range(4)], axis=0)
            out = nt(products[m], weights)
            for pair in range(2):
                kp = 2 * quad + pair
                keep = sub == 2 * kp + lane // 64
                for c in range(2):
                    part = out[c * KL : (c + 1) * KL, pair * 128 : (pair + 1) * 128]
                    row = (m * 2 + c) * 4 + kp
                    rows[row : row + 1, :] = jnp.sum(
                        jnp.where(keep, part, 0.0), axis=0, keepdims=True
                    )
    piece[...] = rows[...].astype(BF16)

    pl.semaphore_wait(barrier, len(near) + 6 + 1)
    sent_modes = []
    for i, distance in enumerate(near):
        sent_modes.append(
            remote(
                piece,
                gathered.at[core, z],
                ag_send.at[i],
                ag_recv.at[z],
                ma=on_z(distance) * 2 + core,
            )
        )
        sent_modes[-1].start()
    gathered[core, z] = piece[...]

    for copy in loads[4:]:
        copy.wait()
    cell = lax.broadcasted_iota(I32, (128, 128), 0).astype(F32).astype(BF16)

    def spread(row):
        return jnp.concatenate([jnp.broadcast_to(row, (16, 128)).astype(BF16)] * 8, axis=0)

    def interpolator(s):
        block = lax.rem(local_s[s], PHI_BLOCKS)
        away = cell - spread(offset[pl.ds(s, 1), :].astype(F32))
        right = fraction[pl.ds(s, 1), :]
        mix = jnp.where(
            away == 0.0,
            spread(1.0 - right),
            jnp.where(away == 1.0, spread(right), jnp.zeros((128, 128), BF16)),
        )
        return nn(phase[block], mix).astype(BF16)

    def interpolator_pair(i, _):
        interp[i] = jnp.concatenate([interpolator(2 * i), interpolator(2 * i + 1)], axis=1)
        return 0

    def modes_of(distance):
        source = on_z(distance)
        came(gathered.at[core, source], ag_send.at[0], ag_recv.at[source]).wait_recv()

    lax.fori_loop(0, EARLY, interpolator_pair, 0, unroll=2)

    for source, onward in ((-4, (4, 3, 2, 1)), (4, (-3, -2, -1))):
        modes_of(source)
        block = gathered.at[core, on_z(source)]
        for distance in onward:
            i = len(sent_modes)
            sent_modes.append(
                remote(
                    block,
                    block,
                    ag_send.at[i],
                    ag_recv.at[on_z(source)],
                    ma=on_z(distance) * 2 + core,
                )
            )
            sent_modes[-1].start()
    lax.fori_loop(EARLY, NSB // 2, interpolator_pair, 0, unroll=2)
    for distance in (3, -3, 2, -2, 1, -1, 5, -5, 6, -6, 7, -7, 8):
        modes_of(distance)
    swap_modes = remote(gathered.at[core], gathered.at[core], agp_send, agp_recv, ma=partner)
    swap_modes.start()
    came(gathered.at[1 - core], agp_send, agp_recv).wait_recv()
    gathered_f[...] = gathered[...].astype(F32).reshape(512, 128)
    for kp in range(4):
        block = gathered_f[pl.ds(kp, 128, stride=4), :].T
        modes[:, 2 * kp, :] = block[:64]
        modes[:, 2 * kp + 1, :] = block[64:]

    def forward(first, rows_at):
        for j in range(0, 16, 2):
            own = []
            for s in (first + j, first + j + 1):
                own.append(modes[owner_s[s] * 2 + lax.div(local_s[s], PHI_BLOCKS)])
            values = nn(jnp.concatenate(own, axis=0).astype(BF16), interp[(first + j) // 2])
            for i in range(2):
                part = values[i * KL : (i + 1) * KL, i * 128 : (i + 1) * 128]
                partial[rows_at + j + i : rows_at + j + i + 1, :] = jnp.sum(
                    turn[first + j + i] * part, axis=0, keepdims=True
                )

    def exchange(chunk, stage, out, into, send, recv):
        x_first = chunk < 2
        use_x = x_first if stage == 0 else not x_first
        mine = x if use_x else y
        copies = []
        for i in range(1, 4):
            peer = along_x(i) if use_x else along_y(i)
            copies.append(
                remote(
                    out.at[chunk],
                    into.at[chunk, mine],
                    send.at[chunk, i],
                    recv.at[chunk, mine],
                    beam=peer,
                )
            )
        return copies

    def collect(chunk, stage, own, into, send, recv):
        x_first = chunk < 2
        use_x = x_first if stage == 0 else not x_first
        mine = x if use_x else y
        total = own
        for i in range(1, 4):
            source = lax.rem(mine + i, 4)
            came(into.at[chunk, source], send.at[chunk, i], recv.at[chunk, source]).wait_recv()
            total = total + into[chunk, source].astype(F32)
        return total

    first_stage = [exchange(c, 0, sum_out, sum_in, s1_send, s1_recv) for c in range(4)]
    second_stage = [exchange(c, 1, sum2_out, sum2_in, s2_send, s2_recv) for c in range(4)]
    sequence = (0, 2, 1, 3)
    for chunk in sequence:
        forward(chunk * 32, 0)
        forward(chunk * 32 + 16, 16)
        sum_out[chunk] = partial[...].astype(BF16)
        for copy in first_stage[chunk]:
            copy.start()
    for chunk in sequence:
        total = collect(chunk, 0, sum_out[chunk].astype(F32), sum_in, s1_send, s1_recv)
        sum2_out[chunk] = total.astype(BF16)
        for copy in second_stage[chunk]:
            copy.start()

    def backward(first, rows_at):
        for j in range(0, 16, 2):
            lhs = []
            for i in (j, j + 1):
                lhs += split(turn[first + i] * filtered[rows_at + i : rows_at + i + 1, :])
            weights = interp[(first + j) // 2]
            weights = jnp.concatenate([weights[:, :128], weights[:, 128:]], axis=0)
            both = nt(jnp.concatenate(lhs, axis=0), weights)
            s = first + j
            gmat[s * KL : (s + 1) * KL, :] = both[:KL, :128] + both[KL : 2 * KL, :128]
            gmat[(s + 1) * KL : (s + 2) * KL, :] = (
                both[2 * KL : 3 * KL, 128:] + both[3 * KL :, 128:]
            )

    for chunk in sequence:
        signal = collect(chunk, 1, sum2_out[chunk].astype(F32), sum2_in, s2_send, s2_recv)
        stamps = (
            chunk * 32 + lax.broadcasted_iota(I32, (32, 128), 0)
        ) * 128 + lax.broadcasted_iota(I32, (32, 128), 1)
        valid = (stamps < count_s[0]).astype(F32)
        filtered[...] = (
            lax.dot_general(
                signal * valid,
                noise[...],
                (((1,), (1,)), ((), ())),
                precision=lax.Precision.HIGHEST,
                preferred_element_type=F32,
            )
            * valid
        )
        backward(chunk * 32, 0)
        backward(chunk * 32 + 16, 16)

    cycles = owner_row[...] * 2 + lax.div(local_row[...], jnp.full((1, NSB), PHI_BLOCKS, I32))
    pick = (lax.broadcasted_iota(I32, (64, 128), 0) == cycles).astype(F32).astype(BF16)
    pick = jnp.concatenate([pick, pick], axis=1)
    for kp in range(4):
        halves = []
        for k in (2 * kp, 2 * kp + 1):
            high, low = split(gmat[pl.ds(k, 128, stride=KL), :])
            halves.append(nn(pick, jnp.concatenate([high, low], axis=0)))
        gout_f[pl.ds(kp, 128, stride=4), :] = jnp.concatenate(halves, axis=0).T

    half_rows = pl.multiple_of(core * 256, 256)
    other_rows = pl.multiple_of((1 - core) * 256, 256)
    swap_grads = remote(gout_f.at[pl.ds(other_rows, 256)], gpair, grp_send, grp_recv, ma=partner)
    swap_grads.start()
    swap_modes.wait_send()
    for copy in sent_modes:
        copy.wait_send()
    came(gpair, grp_send, grp_recv).wait_recv()
    gout[...] = (gout_f[pl.ds(half_rows, 256), :] + gpair[...]).reshape(16, 16, 128).astype(BF16)

    def send_grads(i, _):
        peer = far_z(i)
        to_z(gout.at[peer], gin.at[z], gr_send, gr_recv, peer).start()
        return 0

    lax.fori_loop(0, 15, send_grads, 0)
    for chunk in range(4):
        for copy in first_stage[chunk] + second_stage[chunk]:
            copy.wait_send()
    swap_grads.wait_send()

    def grads_arrive(i, acc):
        source = far_z(14 - i)
        came(gin.at[source], gr_send.at[source], gr_recv.at[source]).wait_recv()
        return acc + gin[source].astype(F32)

    rows[...] = lax.fori_loop(0, 15, grads_arrive, gout[z].astype(F32))

    for m in range(2):
        lhs = []
        for c in range(2):
            for kp in range(4):
                row = (m * 2 + c) * 4 + kp
                spreadout = jnp.broadcast_to(rows[row : row + 1, :], (KL, 128))
                lhs.append(jnp.where(sub == 2 * kp + lane // 64, spreadout, 0.0))
        lhs = jnp.concatenate(
            [jnp.concatenate(lhs[:4], axis=1), jnp.concatenate(lhs[4:], axis=1)], axis=0
        ).astype(BF16)
        weights = jnp.concatenate([wig[k, m] for k in range(KL)], axis=0)
        harm = nn(lhs, weights)
        re, im = harm[:KL], harm[KL:]
        first = jnp.sum(re * beam_re + im * beam_im, axis=0, keepdims=True)
        second = jnp.sum(im * beam_re - re * beam_im, axis=0, keepdims=True)
        for b in range(N_BEAM):
            fin[b, 2 * m : 2 * m + 1, :] = first[:, b * 128 : (b + 1) * 128]
            fin[b, 2 * m + 1 : 2 * m + 2, :] = second[:, b * 128 : (b + 1) * 128]

    def send_final(i, _):
        peer = lax.rem(me_b + 1 + i, N_BEAM)
        to_beam(fin.at[peer], fin_in.at[me_b], fin_send, fin_recv, peer).start()
        return 0

    lax.fori_loop(0, N_BEAM - 1, send_final, 0)

    def sent_grads(i, _):
        peer = far_z(i)
        to_z(gout.at[peer], gin.at[z], gr_send, gr_recv, peer).wait_send()
        return 0

    lax.fori_loop(0, 15, sent_grads, 0)

    def final_arrive(i, acc):
        source = lax.rem(me_b + N_BEAM - 1 - i, N_BEAM)
        came(fin_in.at[source], fin_send.at[source], fin_recv.at[source]).wait_recv()
        return acc + fin_in[source]

    result = lax.fori_loop(0, N_BEAM - 1, final_arrive, fin[me_b])
    out_ref[0] = result[0:2]
    out_ref[1] = result[2:4]

    def sent_final(i, _):
        peer = lax.rem(me_b + 1 + i, N_BEAM)
        to_beam(fin.at[peer], fin_in.at[me_b], fin_send, fin_recv, peer).wait_send()
        return 0

    lax.fori_loop(0, N_BEAM - 1, sent_final, 0)


def local(
    sky_harmonics,
    beam_harmonics,
    wigner,
    order_map,
    block_owner,
    block_local,
    cell_offset,
    cell_fraction,
    beam_angle,
    sample_count,
    noise_weight,
):
    hbm = pl.BlockSpec(memory_space=pl.ANY)
    vmem, smem, dma = pltpu.VMEM, pltpu.SMEM, pltpu.SemaphoreType.DMA
    owner = block_owner.reshape(NSB)
    return pl.pallas_call(
        kernel,
        out_shape=pltpu.VMEM((2, 2, 128), F32),
        in_specs=[hbm] * 3 + [pl.BlockSpec(memory_space=smem)] + [hbm] * 9,
        out_specs=pl.BlockSpec(memory_space=pltpu.VMEM),
        scratch_shapes=[
            smem((NSB,), I32),
            smem((NSB,), I32),
            smem((64,), I32),
            vmem((1, NSB), I32),
            vmem((1, NSB), I32),
            vmem((2, 2, 2048), F32),
            vmem((KL, 2, 2048), F32),
            vmem((KL, 2, 64, 2048), BF16),
            vmem((NSB, 128), I32),
            vmem((NSB, 128), F32),
            vmem((NSB, 128), F32),
            vmem((128, 128), F32),
            vmem((128, 128), I32),
            vmem((PHI_BLOCKS, 128, 128), BF16),
            vmem((NSB, KL, 128), F32),
            vmem((NSB // 2, 128, 256), BF16),
            vmem((16, 128), F32),
            vmem((16, 128), BF16),
            vmem((2, 16, 16, 128), BF16),
            vmem((512, 128), F32),
            vmem((64, KL, 128), F32),
            vmem((32, 128), F32),
            vmem((4, 32, 128), BF16),
            vmem((4, 4, 32, 128), BF16),
            vmem((4, 32, 128), BF16),
            vmem((4, 4, 32, 128), BF16),
            vmem((32, 128), F32),
            vmem((NSB * KL, 128), F32),
            vmem((512, 128), F32),
            vmem((256, 128), F32),
            vmem((16, 16, 128), BF16),
            vmem((16, 16, 128), BF16),
            vmem((N_BEAM, 4, 128), F32),
            vmem((N_BEAM, 4, 128), F32),
            dma((11,)),
            dma((4,)),
            dma((16,)),
            dma((16,)),
            dma,
            dma,
            dma((4, 4)),
            dma((4, 4)),
            dma((4, 4)),
            dma((4, 4)),
            dma,
            dma,
            dma((16,)),
            dma((16,)),
            dma((N_BEAM,)),
            dma((N_BEAM,)),
        ],
        compiler_params=pltpu.CompilerParams(collective_id=0, has_side_effects=True),
        name="normal_operator",
    )(
        owner,
        block_local,
        order_map,
        sample_count,
        owner.reshape(1, NSB),
        block_local.reshape(1, NSB),
        sky_harmonics,
        beam_harmonics,
        wigner,
        cell_offset.reshape(NSB, 128),
        cell_fraction.reshape(NSB, 128),
        beam_angle.reshape(NSB, 128),
        noise_weight,
    )


def solution(mesh):
    return jax.shard_map(
        local,
        mesh=mesh,
        in_specs=(
            P("ma", None, None),
            P("beam", None, None),
            P("beam", "ma", None, None),
            P(),
            P("ma", None),
            P("ma"),
            P("ma"),
            P("ma"),
            P("ma"),
            P("ma"),
            P(),
        ),
        out_specs=P("ma", None, "beam"),
        check_vma=False,
    )
```

```python
import functools
import math

import jax
import jax.numpy as jnp
from jax import lax
from jax.experimental import pallas as pl
from jax.experimental.pallas import tpu as pltpu
from jax.sharding import PartitionSpec as P

F32 = jnp.float32
BF16 = jnp.bfloat16
I32 = jnp.int32

COS_TURNS = (
    0.99999997389483,
    -19.739202931827737,
    64.93907559492132,
    -85.44969773655134,
    60.1656143595228,
    -25.96416606164654,
    6.528151014475474,
)
N_MA = 32
N_BEAM = 16
KL = 8
PHI_BLOCKS = 32
NSB = 128
EARLY = 16


def cos_turns(turns):
    v = turns - jnp.floor(turns + 0.5)
    w = v * v
    acc = jnp.full_like(w, COS_TURNS[-1])
    for coef in COS_TURNS[-2::-1]:
        acc = acc * w + coef
    return acc


def nn(a, b):
    return lax.dot_general(a, b, (((1,), (0,)), ((), ())), preferred_element_type=F32)


def nt(a, b):
    return lax.dot_general(a, b, (((1,), (1,)), ((), ())), preferred_element_type=F32)


def split(x):
    high = x.astype(BF16)
    return high, (x - high.astype(F32)).astype(BF16)


def kernel(
    owner_hbm,
    local_hbm,
    order_hbm,
    count_s,
    owner_row_hbm,
    local_row_hbm,
    sky_hbm,
    beam_hbm,
    wig_hbm,
    offset_hbm,
    fraction_hbm,
    angle_hbm,
    noise_hbm,
    out_ref,
    owner_s,
    local_s,
    order_s,
    owner_row,
    local_row,
    sky,
    beam,
    wig,
    offset,
    fraction,
    angle,
    noise,
    order,
    phase,
    turn,
    interp,
    rows,
    piece,
    gathered,
    gathered_f,
    modes,
    partial,
    sum_out,
    sum_in,
    sum2_out,
    sum2_in,
    filtered,
    gmat,
    gout_f,
    gpair,
    gout,
    gin,
    fin,
    fin_in,
    load_sem,
    wig_sem,
    ag_send,
    ag_recv,
    agp_send,
    agp_recv,
    s1_send,
    s1_recv,
    s2_send,
    s2_recv,
    grp_send,
    grp_recv,
    gr_send,
    gr_recv,
    fin_send,
    fin_recv,
):
    me_a = lax.axis_index("ma")
    me_b = lax.axis_index("beam")
    z = lax.div(me_a, 2)
    core = lax.rem(me_a, 2)
    x = lax.rem(me_b, 4)
    y = lax.div(me_b, 4)

    loads = [
        pltpu.make_async_copy(src, dst, load_sem.at[i])
        for i, (src, dst) in enumerate(
            [
                (order_hbm, order_s),
                (angle_hbm, angle),
                (beam_hbm, beam),
                (sky_hbm, sky),
                (local_hbm, local_s),
                (owner_hbm, owner_s),
                (offset_hbm, offset),
                (fraction_hbm, fraction),
                (owner_row_hbm, owner_row),
                (local_row_hbm, local_row),
                (noise_hbm, noise),
            ]
        )
    ]
    wig_loads = [
        pltpu.make_async_copy(wig_hbm.at[pl.ds(2 * i, 2)], wig.at[pl.ds(2 * i, 2)], wig_sem.at[i])
        for i in range(4)
    ]
    for copy in loads[:4] + wig_loads:
        copy.start()

    barrier = pltpu.get_barrier_semaphore()

    def far_z(i):
        half = (i + 1) // 2
        return lax.rem(z + 16 + 8 + half * (1 - 2 * lax.rem(i, 2)), 16)

    def along_x(i):
        return y * 4 + lax.rem(x + i, 4)

    def along_y(i):
        return lax.rem(y + i, 4) * 4 + x

    def on_z(distance):
        return lax.rem(z + 16 + distance, 16)

    near = (4, -4, 3, -3, 2, -2, 1, -1)
    partner = z * 2 + 1 - core
    for distance in near:
        pl.semaphore_signal(barrier, inc=1, device_id={"ma": on_z(distance) * 2 + core})
    for i in (2, 1, 3):
        pl.semaphore_signal(barrier, inc=1, device_id={"beam": along_x(i)})
        pl.semaphore_signal(barrier, inc=1, device_id={"beam": along_y(i)})
    pl.semaphore_signal(barrier, inc=1, device_id={"ma": partner})
    for copy in loads[4:]:
        copy.start()

    def remote(src, dst, send, recv, **peer):
        return pltpu.make_async_remote_copy(
            src_ref=src, dst_ref=dst, send_sem=send, recv_sem=recv, device_id=peer
        )

    def to_z(src, dst, send, recv, peer):
        return remote(src, dst, send.at[peer], recv.at[z], ma=peer * 2 + core)

    def to_beam(src, dst, send, recv, peer):
        return remote(src, dst, send.at[peer], recv.at[me_b], beam=peer)

    def came(dst, send, recv):
        return remote(dst, dst, send, recv, ma=me_a)

    sub = lax.broadcasted_iota(I32, (KL, 128), 0)
    lane = lax.broadcasted_iota(I32, (KL, 128), 1)

    loads[0].wait()
    for a_core in range(2):
        for a_z in range(16):
            for m in range(2):
                row = (a_core * 16 + a_z) * 4 + m * 2
                order[row : row + 2, :] = jnp.full((2, 128), order_s[(a_z * 2 + a_core) * 2 + m], I32)
    for half in range(2):
        orders = order[half * 64 : half * 64 + 64, :].astype(F32)
        cells = lax.broadcasted_iota(I32, (64, 128), 1).astype(F32) * (1.0 / 4096.0)
        quarter = (lax.broadcasted_iota(I32, (64, 128), 0) % 2).astype(F32) * 0.25
        start = orders * cells + quarter
        step = orders * (1.0 / 32.0)
        step_re = cos_turns(step)
        step_im = cos_turns(step - 0.25)

        def phases(b, carried):
            re, im = carried
            phase[b, half * 64 : half * 64 + 64, :] = re.astype(BF16)
            return re * step_re - im * step_im, im * step_re + re * step_im

        lax.fori_loop(
            0,
            PHI_BLOCKS,
            phases,
            (cos_turns(start) * 0.125, cos_turns(start - 0.25) * 0.125),
            unroll=2,
        )
    loads[1].wait()
    beam_order = me_b * KL + sub
    spin = ((beam_order + 1) // 2).astype(F32)
    back = (beam_order % 2).astype(F32) * 0.25

    def turns_of(s, _):
        around = angle[pl.ds(s, 1), :] * (1.0 / (2.0 * math.pi))
        turn[s] = cos_turns(spin * around - back) * (1.0 / math.sqrt(128.0))
        return 0

    lax.fori_loop(0, NSB, turns_of, 0, unroll=4)

    loads[2].wait()
    loads[3].wait()
    beam_re = beam[:, 0, :]
    beam_im = beam[:, 1, :]
    products = []
    for m in range(2):
        sky_re = sky[m, 0:1, :]
        sky_im = sky[m, 1:2, :]
        products.append(
            jnp.concatenate(
                [sky_re * beam_re - sky_im * beam_im, sky_re * beam_im + sky_im * beam_re], axis=0
            ).astype(BF16)
        )
    for quad in range(2):
        wig_loads[2 * quad].wait()
        wig_loads[2 * quad + 1].wait()
        for m in range(2):
            weights = jnp.concatenate([wig[4 * quad + k, m] for k in range(4)], axis=0)
            out = nt(products[m], weights)
            for pair in range(2):
                kp = 2 * quad + pair
                keep = sub == 2 * kp + lane // 64
                for c in range(2):
                    part = out[c * KL : (c + 1) * KL, pair * 128 : (pair + 1) * 128]
                    row = (m * 2 + c) * 4 + kp
                    rows[row : row + 1, :] = jnp.sum(
                        jnp.where(keep, part, 0.0), axis=0, keepdims=True
                    )
    piece[...] = rows[...].astype(BF16)

    pl.semaphore_wait(barrier, len(near) + 6 + 1)
    sent_modes = []
    for i, distance in enumerate(near):
        sent_modes.append(
            remote(
                piece,
                gathered.at[core, z],
                ag_send.at[i],
                ag_recv.at[z],
                ma=on_z(distance) * 2 + core,
            )
        )
        sent_modes[-1].start()
    gathered[core, z] = piece[...]

    for copy in loads[4:]:
        copy.wait()
    cell = lax.broadcasted_iota(I32, (128, 128), 0).astype(F32).astype(BF16)

    def spread(row):
        return jnp.concatenate([jnp.broadcast_to(row, (16, 128)).astype(BF16)] * 8, axis=0)

    def interpolator(s):
        block = lax.rem(local_s[s], PHI_BLOCKS)
        away = cell - spread(offset[pl.ds(s, 1), :].astype(F32))
        right = fraction[pl.ds(s, 1), :]
        mix = jnp.where(
            away == 0.0,
            spread(1.0 - right),
            jnp.where(away == 1.0, spread(right), jnp.zeros((128, 128), BF16)),
        )
        return nn(phase[block], mix).astype(BF16)

    noise_high, noise_low = split(noise[...])
    noise_twice = jnp.concatenate([noise_high, noise_high], axis=1)

    def interpolator_pair(i, _):
        interp[i] = jnp.concatenate([interpolator(2 * i), interpolator(2 * i + 1)], axis=1)
        return 0

    def modes_of(distance):
        source = on_z(distance)
        came(gathered.at[core, source], ag_send.at[0], ag_recv.at[source]).wait_recv()

    lax.fori_loop(0, EARLY, interpolator_pair, 0, unroll=2)

    for source, onward in ((-4, (4, 3, 2, 1)), (4, (-3, -2, -1))):
        modes_of(source)
        block = gathered.at[core, on_z(source)]
        for distance in onward:
            i = len(sent_modes)
            sent_modes.append(
                remote(
                    block,
                    block,
                    ag_send.at[i],
                    ag_recv.at[on_z(source)],
                    ma=on_z(distance) * 2 + core,
                )
            )
            sent_modes[-1].start()
    lax.fori_loop(EARLY, NSB // 2, interpolator_pair, 0, unroll=2)
    for distance in (3, -3, 2, -2, 1, -1, 5, -5, 6, -6, 7, -7, 8):
        modes_of(distance)
    swap_modes = remote(gathered.at[core], gathered.at[core], agp_send, agp_recv, ma=partner)
    swap_modes.start()
    came(gathered.at[1 - core], agp_send, agp_recv).wait_recv()
    gathered_f[...] = gathered[...].astype(F32).reshape(512, 128)
    for kp in range(4):
        block = gathered_f[pl.ds(kp, 128, stride=4), :].T
        modes[:, 2 * kp, :] = block[:64]
        modes[:, 2 * kp + 1, :] = block[64:]

    def forward(first, rows_at):
        for j in range(0, 16, 2):
            own = []
            for s in (first + j, first + j + 1):
                own.append(modes[owner_s[s] * 2 + lax.div(local_s[s], PHI_BLOCKS)])
            values = nn(jnp.concatenate(own, axis=0).astype(BF16), interp[(first + j) // 2])
            for i in range(2):
                part = values[i * KL : (i + 1) * KL, i * 128 : (i + 1) * 128]
                partial[rows_at + j + i : rows_at + j + i + 1, :] = jnp.sum(
                    turn[first + j + i] * part, axis=0, keepdims=True
                )

    def exchange(chunk, stage, out, into, send, recv):
        x_first = chunk == 0
        use_x = x_first if stage == 0 else not x_first
        mine = x if use_x else y
        copies = []
        for i in range(1, 4):
            peer = along_x(i) if use_x else along_y(i)
            copies.append(
                remote(
                    out.at[chunk],
                    into.at[chunk, mine],
                    send.at[chunk, i],
                    recv.at[chunk, mine],
                    beam=peer,
                )
            )
        return copies

    def collect(chunk, stage, own, into, send, recv):
        x_first = chunk == 0
        use_x = x_first if stage == 0 else not x_first
        mine = x if use_x else y
        total = own
        for i in range(1, 4):
            source = lax.rem(mine + i, 4)
            came(into.at[chunk, source], send.at[chunk, i], recv.at[chunk, source]).wait_recv()
            total = total + into[chunk, source].astype(F32)
        return total

    first_stage = [exchange(c, 0, sum_out, sum_in, s1_send, s1_recv) for c in range(2)]
    second_stage = [exchange(c, 1, sum2_out, sum2_in, s2_send, s2_recv) for c in range(2)]
    sequence = (0, 1)
    for chunk in sequence:
        for rows_at in range(0, 64, 16):
            forward(chunk * 64 + rows_at, rows_at)
        sum_out[chunk] = partial[...].astype(BF16)
        for copy in first_stage[chunk]:
            copy.start()
    for chunk in sequence:
        total = collect(chunk, 0, sum_out[chunk].astype(F32), sum_in, s1_send, s1_recv)
        sum2_out[chunk] = total.astype(BF16)
        for copy in second_stage[chunk]:
            copy.start()

    def backward(first, rows_at):
        for j in range(0, 16, 2):
            lhs = []
            for i in (j, j + 1):
                lhs.append(turn[first + i] * filtered[rows_at + i : rows_at + i + 1, :])
            weights = interp[(first + j) // 2]
            weights = jnp.concatenate([weights[:, :128], weights[:, 128:]], axis=0)
            both = nt(jnp.concatenate(lhs, axis=0).astype(BF16), weights)
            s = first + j
            gmat[s * KL : (s + 1) * KL, :] = both[:KL, :128]
            gmat[(s + 1) * KL : (s + 2) * KL, :] = both[KL:, 128:]

    for chunk in sequence:
        signal = collect(chunk, 1, sum2_out[chunk].astype(F32), sum2_in, s2_send, s2_recv)
        stamps = (
            chunk * 64 + lax.broadcasted_iota(I32, (64, 128), 0)
        ) * 128 + lax.broadcasted_iota(I32, (64, 128), 1)
        valid = (stamps < count_s[0]).astype(F32)
        high, low = split(signal * valid)
        mixed = nt(jnp.concatenate([high, low], axis=1), noise_twice) + nt(high, noise_low)
        filtered[...] = mixed * valid
        for rows_at in range(0, 64, 16):
            backward(chunk * 64 + rows_at, rows_at)

    cycles = owner_row[...] * 2 + lax.div(local_row[...], jnp.full((1, NSB), PHI_BLOCKS, I32))
    pick = (lax.broadcasted_iota(I32, (64, 128), 0) == cycles).astype(F32).astype(BF16)
    pick = jnp.concatenate([pick, pick], axis=1)
    for kp in range(4):
        halves = []
        for k in (2 * kp, 2 * kp + 1):
            high, low = split(gmat[pl.ds(k, 128, stride=KL), :])
            halves.append(nn(pick, jnp.concatenate([high, low], axis=0)))
        gout_f[pl.ds(kp, 128, stride=4), :] = jnp.concatenate(halves, axis=0).T

    half_rows = pl.multiple_of(core * 256, 256)
    other_rows = pl.multiple_of((1 - core) * 256, 256)
    swap_grads = remote(gout_f.at[pl.ds(other_rows, 256)], gpair, grp_send, grp_recv, ma=partner)
    swap_grads.start()
    swap_modes.wait_send()
    for copy in sent_modes:
        copy.wait_send()
    came(gpair, grp_send, grp_recv).wait_recv()
    gout[...] = (gout_f[pl.ds(half_rows, 256), :] + gpair[...]).reshape(16, 16, 128).astype(BF16)

    def send_grads(i, _):
        peer = far_z(i)
        to_z(gout.at[peer], gin.at[z], gr_send, gr_recv, peer).start()
        return 0

    lax.fori_loop(0, 15, send_grads, 0)
    for chunk in range(2):
        for copy in first_stage[chunk] + second_stage[chunk]:
            copy.wait_send()
    swap_grads.wait_send()

    def grads_arrive(i, acc):
        source = far_z(14 - i)
        came(gin.at[source], gr_send.at[source], gr_recv.at[source]).wait_recv()
        return acc + gin[source].astype(F32)

    rows[...] = lax.fori_loop(0, 15, grads_arrive, gout[z].astype(F32))

    for m in range(2):
        lhs = []
        for c in range(2):
            for kp in range(4):
                row = (m * 2 + c) * 4 + kp
                spreadout = jnp.broadcast_to(rows[row : row + 1, :], (KL, 128))
                lhs.append(jnp.where(sub == 2 * kp + lane // 64, spreadout, 0.0))
        lhs = jnp.concatenate(
            [jnp.concatenate(lhs[:4], axis=1), jnp.concatenate(lhs[4:], axis=1)], axis=0
        ).astype(BF16)
        weights = jnp.concatenate([wig[k, m] for k in range(KL)], axis=0)
        harm = nn(lhs, weights)
        re, im = harm[:KL], harm[KL:]
        first = jnp.sum(re * beam_re + im * beam_im, axis=0, keepdims=True)
        second = jnp.sum(im * beam_re - re * beam_im, axis=0, keepdims=True)
        for b in range(N_BEAM):
            fin[b, 2 * m : 2 * m + 1, :] = first[:, b * 128 : (b + 1) * 128]
            fin[b, 2 * m + 1 : 2 * m + 2, :] = second[:, b * 128 : (b + 1) * 128]

    def send_final(i, _):
        peer = lax.rem(me_b + 1 + i, N_BEAM)
        to_beam(fin.at[peer], fin_in.at[me_b], fin_send, fin_recv, peer).start()
        return 0

    lax.fori_loop(0, N_BEAM - 1, send_final, 0)

    def sent_grads(i, _):
        peer = far_z(i)
        to_z(gout.at[peer], gin.at[z], gr_send, gr_recv, peer).wait_send()
        return 0

    lax.fori_loop(0, 15, sent_grads, 0)

    def final_arrive(i, acc):
        source = lax.rem(me_b + N_BEAM - 1 - i, N_BEAM)
        came(fin_in.at[source], fin_send.at[source], fin_recv.at[source]).wait_recv()
        return acc + fin_in[source]

    result = lax.fori_loop(0, N_BEAM - 1, final_arrive, fin[me_b])
    out_ref[0] = result[0:2]
    out_ref[1] = result[2:4]

    def sent_final(i, _):
        peer = lax.rem(me_b + 1 + i, N_BEAM)
        to_beam(fin.at[peer], fin_in.at[me_b], fin_send, fin_recv, peer).wait_send()
        return 0

    lax.fori_loop(0, N_BEAM - 1, sent_final, 0)


def local(
    sky_harmonics,
    beam_harmonics,
    wigner,
    order_map,
    block_owner,
    block_local,
    cell_offset,
    cell_fraction,
    beam_angle,
    sample_count,
    noise_weight,
):
    hbm = pl.BlockSpec(memory_space=pl.ANY)
    vmem, smem, dma = pltpu.VMEM, pltpu.SMEM, pltpu.SemaphoreType.DMA
    owner = block_owner.reshape(NSB)
    return pl.pallas_call(
        kernel,
        out_shape=pltpu.VMEM((2, 2, 128), F32),
        in_specs=[hbm] * 3 + [pl.BlockSpec(memory_space=smem)] + [hbm] * 9,
        out_specs=pl.BlockSpec(memory_space=pltpu.VMEM),
        scratch_shapes=[
            smem((NSB,), I32),
            smem((NSB,), I32),
            smem((64,), I32),
            vmem((1, NSB), I32),
            vmem((1, NSB), I32),
            vmem((2, 2, 2048), F32),
            vmem((KL, 2, 2048), F32),
            vmem((KL, 2, 64, 2048), BF16),
            vmem((NSB, 128), I32),
            vmem((NSB, 128), F32),
            vmem((NSB, 128), F32),
            vmem((128, 128), F32),
            vmem((128, 128), I32),
            vmem((PHI_BLOCKS, 128, 128), BF16),
            vmem((NSB, KL, 128), F32),
            vmem((NSB // 2, 128, 256), BF16),
            vmem((16, 128), F32),
            vmem((16, 128), BF16),
            vmem((2, 16, 16, 128), BF16),
            vmem((512, 128), F32),
            vmem((64, KL, 128), F32),
            vmem((64, 128), F32),
            vmem((2, 64, 128), BF16),
            vmem((2, 4, 64, 128), BF16),
            vmem((2, 64, 128), BF16),
            vmem((2, 4, 64, 128), BF16),
            vmem((64, 128), F32),
            vmem((NSB * KL, 128), F32),
            vmem((512, 128), F32),
            vmem((256, 128), F32),
            vmem((16, 16, 128), BF16),
            vmem((16, 16, 128), BF16),
            vmem((N_BEAM, 4, 128), F32),
            vmem((N_BEAM, 4, 128), F32),
            dma((11,)),
            dma((4,)),
            dma((16,)),
            dma((16,)),
            dma,
            dma,
            dma((2, 4)),
            dma((2, 4)),
            dma((2, 4)),
            dma((2, 4)),
            dma,
            dma,
            dma((16,)),
            dma((16,)),
            dma((N_BEAM,)),
            dma((N_BEAM,)),
        ],
        compiler_params=pltpu.CompilerParams(collective_id=0, has_side_effects=True),
        name="normal_operator",
    )(
        owner,
        block_local,
        order_map,
        sample_count,
        owner.reshape(1, NSB),
        block_local.reshape(1, NSB),
        sky_harmonics,
        beam_harmonics,
        wigner,
        cell_offset.reshape(NSB, 128),
        cell_fraction.reshape(NSB, 128),
        beam_angle.reshape(NSB, 128),
        noise_weight,
    )


def solution(mesh):
    return jax.shard_map(
        local,
        mesh=mesh,
        in_specs=(
            P("ma", None, None),
            P("beam", None, None),
            P("beam", "ma", None, None),
            P(),
            P("ma", None),
            P("ma"),
            P("ma"),
            P("ma"),
            P("ma"),
            P("ma"),
            P(),
        ),
        out_specs=P("ma", None, "beam"),
        check_vma=False,
    )
```

```python
import functools
import math

import jax
import jax.numpy as jnp
from jax import lax
from jax.experimental import pallas as pl
from jax.experimental.pallas import tpu as pltpu
from jax.sharding import PartitionSpec as P

F32 = jnp.float32
BF16 = jnp.bfloat16
I32 = jnp.int32

COS_TURNS = (
    0.99999997389483,
    -19.739202931827737,
    64.93907559492132,
    -85.44969773655134,
    60.1656143595228,
    -25.96416606164654,
    6.528151014475474,
)
N_MA = 32
N_BEAM = 16
KL = 8
PHI_BLOCKS = 32
NSB = 128
EARLY = 16


def cos_turns(turns):
    v = turns - jnp.floor(turns + 0.5)
    w = v * v
    acc = jnp.full_like(w, COS_TURNS[-1])
    for coef in COS_TURNS[-2::-1]:
        acc = acc * w + coef
    return acc


def nn(a, b):
    return lax.dot_general(a, b, (((1,), (0,)), ((), ())), preferred_element_type=F32)


def nt(a, b):
    return lax.dot_general(a, b, (((1,), (1,)), ((), ())), preferred_element_type=F32)


def split(x):
    high = x.astype(BF16)
    return high, (x - high.astype(F32)).astype(BF16)


def kernel(
    owner_hbm,
    local_hbm,
    order_hbm,
    count_s,
    owner_row_hbm,
    local_row_hbm,
    sky_hbm,
    beam_hbm,
    wig_hbm,
    offset_hbm,
    fraction_hbm,
    angle_hbm,
    noise_hbm,
    out_ref,
    owner_s,
    local_s,
    order_s,
    owner_row,
    local_row,
    sky,
    beam,
    wig,
    offset,
    fraction,
    angle,
    noise,
    order,
    phase,
    turn,
    interp,
    rows,
    piece,
    gathered,
    gathered_f,
    modes,
    partial,
    sum_out,
    sum_in,
    sum2_out,
    sum2_in,
    filtered,
    gmat,
    gout_f,
    gpair,
    gout,
    gin,
    fin,
    fin_in,
    load_sem,
    wig_sem,
    ag_send,
    ag_recv,
    agp_send,
    agp_recv,
    s1_send,
    s1_recv,
    s2_send,
    s2_recv,
    grp_send,
    grp_recv,
    gr_send,
    gr_recv,
    fin_send,
    fin_recv,
):
    me_a = lax.axis_index("ma")
    me_b = lax.axis_index("beam")
    z = lax.div(me_a, 2)
    core = lax.rem(me_a, 2)
    x = lax.rem(me_b, 4)
    y = lax.div(me_b, 4)

    loads = [
        pltpu.make_async_copy(src, dst, load_sem.at[i])
        for i, (src, dst) in enumerate(
            [
                (order_hbm, order_s),
                (angle_hbm, angle),
                (beam_hbm, beam),
                (sky_hbm, sky),
                (local_hbm, local_s),
                (owner_hbm, owner_s),
                (offset_hbm, offset),
                (fraction_hbm, fraction),
                (owner_row_hbm, owner_row),
                (local_row_hbm, local_row),
                (noise_hbm, noise),
            ]
        )
    ]
    wig_loads = [
        pltpu.make_async_copy(wig_hbm.at[pl.ds(2 * i, 2)], wig.at[pl.ds(2 * i, 2)], wig_sem.at[i])
        for i in range(4)
    ]
    for copy in loads[:4] + wig_loads:
        copy.start()

    barrier = pltpu.get_barrier_semaphore()

    def far_z(i):
        half = (i + 1) // 2
        return lax.rem(z + 16 + 8 + half * (1 - 2 * lax.rem(i, 2)), 16)

    def along_x(i):
        return y * 4 + lax.rem(x + i, 4)

    def along_y(i):
        return lax.rem(y + i, 4) * 4 + x

    def on_z(distance):
        return lax.rem(z + 16 + distance, 16)

    near = (4, -4, 3, -3, 2, -2, 1, -1)
    partner = z * 2 + 1 - core
    for distance in near:
        pl.semaphore_signal(barrier, inc=1, device_id={"ma": on_z(distance) * 2 + core})
    for i in (2, 1, 3):
        pl.semaphore_signal(barrier, inc=1, device_id={"beam": along_x(i)})
        pl.semaphore_signal(barrier, inc=1, device_id={"beam": along_y(i)})
    pl.semaphore_signal(barrier, inc=1, device_id={"ma": partner})
    for copy in loads[4:]:
        copy.start()

    def remote(src, dst, send, recv, **peer):
        return pltpu.make_async_remote_copy(
            src_ref=src, dst_ref=dst, send_sem=send, recv_sem=recv, device_id=peer
        )

    def to_z(src, dst, send, recv, peer):
        return remote(src, dst, send.at[peer], recv.at[z], ma=peer * 2 + core)

    def to_beam(src, dst, send, recv, peer):
        return remote(src, dst, send.at[peer], recv.at[me_b], beam=peer)

    def came(dst, send, recv):
        return remote(dst, dst, send, recv, ma=me_a)

    sub = lax.broadcasted_iota(I32, (KL, 128), 0)
    lane = lax.broadcasted_iota(I32, (KL, 128), 1)

    loads[0].wait()
    for a_core in range(2):
        for a_z in range(16):
            for m in range(2):
                row = (a_core * 16 + a_z) * 4 + m * 2
                order[row : row + 2, :] = jnp.full((2, 128), order_s[(a_z * 2 + a_core) * 2 + m], I32)
    for half in range(2):
        orders = order[half * 64 : half * 64 + 64, :].astype(F32)
        cells = lax.broadcasted_iota(I32, (64, 128), 1).astype(F32) * (1.0 / 4096.0)
        quarter = (lax.broadcasted_iota(I32, (64, 128), 0) % 2).astype(F32) * 0.25
        start = orders * cells + quarter
        step = orders * (1.0 / 32.0)
        step_re = cos_turns(step)
        step_im = cos_turns(step - 0.25)

        def phases(b, carried):
            re, im = carried
            phase[b, half * 64 : half * 64 + 64, :] = re.astype(BF16)
            return re * step_re - im * step_im, im * step_re + re * step_im

        lax.fori_loop(
            0,
            PHI_BLOCKS,
            phases,
            (cos_turns(start) * 0.125, cos_turns(start - 0.25) * 0.125),
            unroll=2,
        )
    loads[1].wait()
    beam_order = me_b * KL + sub
    spin = ((beam_order + 1) // 2).astype(F32)
    back = (beam_order % 2).astype(F32) * 0.25

    def turns_of(s, _):
        around = angle[pl.ds(s, 1), :] * (1.0 / (2.0 * math.pi))
        turn[s] = cos_turns(spin * around - back) * (1.0 / math.sqrt(128.0))
        return 0

    lax.fori_loop(0, NSB, turns_of, 0, unroll=4)

    loads[2].wait()
    loads[3].wait()
    beam_re = beam[:, 0, :]
    beam_im = beam[:, 1, :]
    products = []
    for m in range(2):
        sky_re = sky[m, 0:1, :]
        sky_im = sky[m, 1:2, :]
        products.append(
            jnp.concatenate(
                [sky_re * beam_re - sky_im * beam_im, sky_re * beam_im + sky_im * beam_re], axis=0
            ).astype(BF16)
        )
    for quad in range(2):
        wig_loads[2 * quad].wait()
        wig_loads[2 * quad + 1].wait()
        for m in range(2):
            weights = jnp.concatenate([wig[4 * quad + k, m] for k in range(4)], axis=0)
            out = nt(products[m], weights)
            for pair in range(2):
                kp = 2 * quad + pair
                keep = sub == 2 * kp + lane // 64
                for c in range(2):
                    part = out[c * KL : (c + 1) * KL, pair * 128 : (pair + 1) * 128]
                    row = (m * 2 + c) * 4 + kp
                    rows[row : row + 1, :] = jnp.sum(
                        jnp.where(keep, part, 0.0), axis=0, keepdims=True
                    )
    piece[...] = rows[...].astype(BF16)

    pl.semaphore_wait(barrier, len(near) + 6 + 1)
    sent_modes = []
    for i, distance in enumerate(near):
        sent_modes.append(
            remote(
                piece,
                gathered.at[core, z],
                ag_send.at[i],
                ag_recv.at[z],
                ma=on_z(distance) * 2 + core,
            )
        )
        sent_modes[-1].start()
    gathered[core, z] = piece[...]

    for copy in loads[4:]:
        copy.wait()
    cell = lax.broadcasted_iota(I32, (128, 128), 0).astype(F32).astype(BF16)

    def spread(row):
        return jnp.concatenate([jnp.broadcast_to(row, (16, 128)).astype(BF16)] * 8, axis=0)

    def interpolator(s):
        block = lax.rem(local_s[s], PHI_BLOCKS)
        away = cell - spread(offset[pl.ds(s, 1), :].astype(F32))
        right = fraction[pl.ds(s, 1), :]
        mix = jnp.where(
            away == 0.0,
            spread(1.0 - right),
            jnp.where(away == 1.0, spread(right), jnp.zeros((128, 128), BF16)),
        )
        return nn(phase[block], mix).astype(BF16)

    noise_high, noise_low = split(noise[...])
    noise_twice = jnp.concatenate([noise_high, noise_high], axis=1)

    def interpolator_pair(i, _):
        interp[i] = jnp.concatenate([interpolator(2 * i), interpolator(2 * i + 1)], axis=1)
        return 0

    def modes_of(distance):
        source = on_z(distance)
        came(gathered.at[core, source], ag_send.at[0], ag_recv.at[source]).wait_recv()

    lax.fori_loop(0, EARLY, interpolator_pair, 0, unroll=2)

    for source, onward in ((-4, (4, 3, 2, 1)), (4, (-3, -2, -1))):
        modes_of(source)
        block = gathered.at[core, on_z(source)]
        for distance in onward:
            i = len(sent_modes)
            sent_modes.append(
                remote(
                    block,
                    block,
                    ag_send.at[i],
                    ag_recv.at[on_z(source)],
                    ma=on_z(distance) * 2 + core,
                )
            )
            sent_modes[-1].start()
    lax.fori_loop(EARLY, NSB // 2, interpolator_pair, 0, unroll=2)
    for distance in (3, -3, 2, -2, 1, -1, 5, -5, 6, -6, 7, -7, 8):
        modes_of(distance)
    swap_modes = remote(gathered.at[core], gathered.at[core], agp_send, agp_recv, ma=partner)
    swap_modes.start()
    came(gathered.at[1 - core], agp_send, agp_recv).wait_recv()
    gathered_f[...] = gathered[...].astype(F32).reshape(512, 128)
    for kp in range(4):
        block = gathered_f[pl.ds(kp, 128, stride=4), :].T
        modes[:, 2 * kp, :] = block[:64]
        modes[:, 2 * kp + 1, :] = block[64:]

    def forward(first, rows_at):
        for j in range(0, 16, 2):
            own = []
            for s in (first + j, first + j + 1):
                own.append(modes[owner_s[s] * 2 + lax.div(local_s[s], PHI_BLOCKS)])
            values = nn(jnp.concatenate(own, axis=0).astype(BF16), interp[(first + j) // 2])
            for i in range(2):
                part = values[i * KL : (i + 1) * KL, i * 128 : (i + 1) * 128]
                partial[rows_at + j + i : rows_at + j + i + 1, :] = jnp.sum(
                    turn[first + j + i] * part, axis=0, keepdims=True
                )

    def exchange(chunk, stage, out, into, send, recv):
        x_first = chunk == 0
        use_x = x_first if stage == 0 else not x_first
        mine = x if use_x else y
        copies = []
        for i in range(1, 4):
            peer = along_x(i) if use_x else along_y(i)
            copies.append(
                remote(
                    out.at[chunk],
                    into.at[chunk, mine],
                    send.at[chunk, i],
                    recv.at[chunk, mine],
                    beam=peer,
                )
            )
        return copies

    def collect(chunk, stage, own, into, send, recv):
        x_first = chunk == 0
        use_x = x_first if stage == 0 else not x_first
        mine = x if use_x else y
        total = own
        for i in range(1, 4):
            source = lax.rem(mine + i, 4)
            came(into.at[chunk, source], send.at[chunk, i], recv.at[chunk, source]).wait_recv()
            total = total + into[chunk, source].astype(F32)
        return total

    first_stage = [exchange(c, 0, sum_out, sum_in, s1_send, s1_recv) for c in range(2)]
    second_stage = [exchange(c, 1, sum2_out, sum2_in, s2_send, s2_recv) for c in range(2)]
    sequence = (0, 1)
    for chunk in sequence:
        for rows_at in range(0, 64, 16):
            forward(chunk * 64 + rows_at, rows_at)
        sum_out[chunk] = partial[...].astype(BF16)
        for copy in first_stage[chunk]:
            copy.start()
    for chunk in sequence:
        total = collect(chunk, 0, sum_out[chunk].astype(F32), sum_in, s1_send, s1_recv)
        sum2_out[chunk] = total.astype(BF16)
        for copy in second_stage[chunk]:
            copy.start()

    def backward(first, rows_at):
        for j in range(0, 16, 2):
            lhs = []
            for i in (j, j + 1):
                lhs.append(turn[first + i] * filtered[rows_at + i : rows_at + i + 1, :])
            weights = interp[(first + j) // 2]
            weights = jnp.concatenate([weights[:, :128], weights[:, 128:]], axis=0)
            both = nt(jnp.concatenate(lhs, axis=0).astype(BF16), weights)
            s = first + j
            gmat[s * KL : (s + 1) * KL, :] = both[:KL, :128]
            gmat[(s + 1) * KL : (s + 2) * KL, :] = both[KL:, 128:]

    for chunk in sequence:
        signal = collect(chunk, 1, sum2_out[chunk].astype(F32), sum2_in, s2_send, s2_recv)
        stamps = (
            chunk * 64 + lax.broadcasted_iota(I32, (64, 128), 0)
        ) * 128 + lax.broadcasted_iota(I32, (64, 128), 1)
        valid = (stamps < count_s[0]).astype(F32)
        high, low = split(signal * valid)
        mixed = nt(jnp.concatenate([high, low], axis=1), noise_twice) + nt(high, noise_low)
        filtered[...] = mixed * valid
        for rows_at in range(0, 64, 16):
            backward(chunk * 64 + rows_at, rows_at)

    cycles = owner_row[...] * 2 + lax.div(local_row[...], jnp.full((1, NSB), PHI_BLOCKS, I32))
    pick = (lax.broadcasted_iota(I32, (64, 128), 0) == cycles).astype(F32).astype(BF16)
    pick = jnp.concatenate([pick, pick], axis=1)
    for kp in range(4):
        halves = []
        for k in (2 * kp, 2 * kp + 1):
            high, low = split(gmat[pl.ds(k, 128, stride=KL), :])
            halves.append(nn(pick, jnp.concatenate([high, low], axis=0)))
        gout_f[pl.ds(kp, 128, stride=4), :] = jnp.concatenate(halves, axis=0).T

    half_rows = pl.multiple_of(core * 256, 256)
    other_rows = pl.multiple_of((1 - core) * 256, 256)
    swap_grads = remote(gout_f.at[pl.ds(other_rows, 256)], gpair, grp_send, grp_recv, ma=partner)
    swap_grads.start()
    swap_modes.wait_send()
    for copy in sent_modes:
        copy.wait_send()
    came(gpair, grp_send, grp_recv).wait_recv()
    gout[...] = (gout_f[pl.ds(half_rows, 256), :] + gpair[...]).reshape(16, 16, 128).astype(BF16)

    for distance in (8, 7, -7, 6, -6, 5, -5, 4, -4, 3, -3, 2, -2, 1, -1):
        peer = on_z(distance)
        to_z(gout.at[peer], gin.at[z], gr_send, gr_recv, peer).start()
    for chunk in range(2):
        for copy in first_stage[chunk] + second_stage[chunk]:
            copy.wait_send()
    swap_grads.wait_send()

    def grads_arrive(i, acc):
        source = far_z(14 - i)
        came(gin.at[source], gr_send.at[source], gr_recv.at[source]).wait_recv()
        return acc + gin[source].astype(F32)

    rows[...] = lax.fori_loop(0, 15, grads_arrive, gout[z].astype(F32))

    for m in range(2):
        lhs = []
        for c in range(2):
            for kp in range(4):
                row = (m * 2 + c) * 4 + kp
                spreadout = jnp.broadcast_to(rows[row : row + 1, :], (KL, 128))
                lhs.append(jnp.where(sub == 2 * kp + lane // 64, spreadout, 0.0))
        lhs = jnp.concatenate(
            [jnp.concatenate(lhs[:4], axis=1), jnp.concatenate(lhs[4:], axis=1)], axis=0
        ).astype(BF16)
        weights = jnp.concatenate([wig[k, m] for k in range(KL)], axis=0)
        harm = nn(lhs, weights)
        re, im = harm[:KL], harm[KL:]
        first = jnp.sum(re * beam_re + im * beam_im, axis=0, keepdims=True)
        second = jnp.sum(im * beam_re - re * beam_im, axis=0, keepdims=True)
        for b in range(N_BEAM):
            fin[b, 2 * m : 2 * m + 1, :] = first[:, b * 128 : (b + 1) * 128]
            fin[b, 2 * m + 1 : 2 * m + 2, :] = second[:, b * 128 : (b + 1) * 128]

    steps = sorted(
        ((dx, dy) for dx in range(4) for dy in range(4) if dx or dy),
        key=lambda d: -(min(d[0], 4 - d[0]) + min(d[1], 4 - d[1])),
    )
    final_copies = []
    for dx, dy in steps:
        peer = lax.rem(y + dy, 4) * 4 + lax.rem(x + dx, 4)
        final_copies.append(to_beam(fin.at[peer], fin_in.at[me_b], fin_send, fin_recv, peer))
        final_copies[-1].start()

    def sent_grads(i, _):
        peer = far_z(i)
        to_z(gout.at[peer], gin.at[z], gr_send, gr_recv, peer).wait_send()
        return 0

    lax.fori_loop(0, 15, sent_grads, 0)

    for copy in final_copies:
        copy.wait_send()

    def final_arrive(i, acc):
        source = lax.rem(me_b + N_BEAM - 1 - i, N_BEAM)
        came(fin_in.at[source], fin_send.at[source], fin_recv.at[source]).wait_recv()
        return acc + fin_in[source]

    result = lax.fori_loop(0, N_BEAM - 1, final_arrive, fin[me_b])
    out_ref[0] = result[0:2]
    out_ref[1] = result[2:4]


def local(
    sky_harmonics,
    beam_harmonics,
    wigner,
    order_map,
    block_owner,
    block_local,
    cell_offset,
    cell_fraction,
    beam_angle,
    sample_count,
    noise_weight,
):
    hbm = pl.BlockSpec(memory_space=pl.ANY)
    vmem, smem, dma = pltpu.VMEM, pltpu.SMEM, pltpu.SemaphoreType.DMA
    owner = block_owner.reshape(NSB)
    return pl.pallas_call(
        kernel,
        out_shape=pltpu.VMEM((2, 2, 128), F32),
        in_specs=[hbm] * 3 + [pl.BlockSpec(memory_space=smem)] + [hbm] * 9,
        out_specs=pl.BlockSpec(memory_space=pltpu.VMEM),
        scratch_shapes=[
            smem((NSB,), I32),
            smem((NSB,), I32),
            smem((64,), I32),
            vmem((1, NSB), I32),
            vmem((1, NSB), I32),
            vmem((2, 2, 2048), F32),
            vmem((KL, 2, 2048), F32),
            vmem((KL, 2, 64, 2048), BF16),
            vmem((NSB, 128), I32),
            vmem((NSB, 128), F32),
            vmem((NSB, 128), F32),
            vmem((128, 128), F32),
            vmem((128, 128), I32),
            vmem((PHI_BLOCKS, 128, 128), BF16),
            vmem((NSB, KL, 128), F32),
            vmem((NSB // 2, 128, 256), BF16),
            vmem((16, 128), F32),
            vmem((16, 128), BF16),
            vmem((2, 16, 16, 128), BF16),
            vmem((512, 128), F32),
            vmem((64, KL, 128), F32),
            vmem((64, 128), F32),
            vmem((2, 64, 128), BF16),
            vmem((2, 4, 64, 128), BF16),
            vmem((2, 64, 128), BF16),
            vmem((2, 4, 64, 128), BF16),
            vmem((64, 128), F32),
            vmem((NSB * KL, 128), F32),
            vmem((512, 128), F32),
            vmem((256, 128), F32),
            vmem((16, 16, 128), BF16),
            vmem((16, 16, 128), BF16),
            vmem((N_BEAM, 4, 128), F32),
            vmem((N_BEAM, 4, 128), F32),
            dma((11,)),
            dma((4,)),
            dma((16,)),
            dma((16,)),
            dma,
            dma,
            dma((2, 4)),
            dma((2, 4)),
            dma((2, 4)),
            dma((2, 4)),
            dma,
            dma,
            dma((16,)),
            dma((16,)),
            dma((N_BEAM,)),
            dma((N_BEAM,)),
        ],
        compiler_params=pltpu.CompilerParams(collective_id=0, has_side_effects=True),
        name="normal_operator",
    )(
        owner,
        block_local,
        order_map,
        sample_count,
        owner.reshape(1, NSB),
        block_local.reshape(1, NSB),
        sky_harmonics,
        beam_harmonics,
        wigner,
        cell_offset.reshape(NSB, 128),
        cell_fraction.reshape(NSB, 128),
        beam_angle.reshape(NSB, 128),
        noise_weight,
    )


def solution(mesh):
    return jax.shard_map(
        local,
        mesh=mesh,
        in_specs=(
            P("ma", None, None),
            P("beam", None, None),
            P("beam", "ma", None, None),
            P(),
            P("ma", None),
            P("ma"),
            P("ma"),
            P("ma"),
            P("ma"),
            P("ma"),
            P(),
        ),
        out_specs=P("ma", None, "beam"),
        check_vma=False,
    )
```
